32 devices in a mesh: seq: 4 (over y, x), col: 8 (over z, core).
Axes of the slice: x: 2, y: 2, z: 4, core: 2. Of those that a mesh axis runs over, the one named last changes fastest.
Arguments:
- alignment: bfloat16 [32, 128, 256], P('seq', 'col')
- row_query: bfloat16 [256, 128], replicated
- row_key: bfloat16 [256, 128], replicated
- row_value: bfloat16 [256, 128], replicated, may hold values from -0.375 to 0.375
- row_output: bfloat16 [128, 256], replicated, may hold values from -0.5 to 0.5
- column_query: bfloat16 [256, 128], replicated
- column_key: bfloat16 [256, 128], replicated
- column_value: bfloat16 [256, 128], replicated, may hold values from -0.375 to 0.375
- column_output: bfloat16 [128, 256], replicated, may hold values from -0.5 to 0.5
Outputs:
- row_update: bfloat16 [32, 128, 256], P('seq', 'col')
- layer_output: bfloat16 [32, 128, 256], P('seq', 'col')
The draws below stay inside these ranges and needn't reach their ends.
All inputs are finite; a program needn't handle non-finite values.
Results may differ from the reference program's by a relative error of at most 0.014.
Values may be sent and summed in bfloat16 or wider, within the bound.
No kernel may reach another device: no remote copies, remote signals or barrier semaphores. Data moves between devices by JAX's collectives and lax.ppermute only.
A program may use at most 64 MiB of HBM per device.

```python
import jax
import jax.numpy as jnp
from jax import lax

D = 256
HEADS = 4
HEAD_DIM = 32
SEQS = 32
COLUMNS = 128
INNER = 128


def draw_alignment(key, part):
    base_key = jax.random.fold_in(key, 101)
    first = jax.random.fold_in(base_key, 0)
    fifth = jax.random.fold_in(base_key, 4)
    shape = (SEQS, COLUMNS, D)
    position = jnp.arange(SEQS, dtype=jnp.float32) / float(max(SEQS - 1, 1))
    share = 0.1 + 0.8 * position
    common = jax.random.normal(fifth, (COLUMNS, D), jnp.float32)
    noise = jax.random.normal(first, shape, jnp.float32)
    field = jnp.sqrt(share)[:, None, None] * common[None, :, :] + jnp.sqrt(1.0 - share)[:, None, None] * noise
    return jnp.clip(field, -6.0, 6.0).astype(jnp.bfloat16)


def attention_pair(key, salt):
    pair_key = jax.random.fold_in(key, salt)
    first, second = jax.random.split(pair_key, 2)
    query = jnp.clip(jax.random.normal(first, (D, INNER), jnp.float32), -6.0, 6.0) * D ** (-0.5)
    drawn = jnp.clip(jax.random.normal(second, (D, INNER), jnp.float32), -6.0, 6.0) * D ** (-0.5)
    return (query, drawn)


def draw_row_query(key, part):
    query, drawn = attention_pair(key, 201)
    return query.astype(jnp.bfloat16)


def draw_row_key(key, part):
    query, drawn = attention_pair(key, 201)
    weight = drawn
    return weight.astype(jnp.bfloat16)


def draw_column_query(key, part):
    query, drawn = attention_pair(key, 307)
    return query.astype(jnp.bfloat16)


def draw_column_key(key, part):
    query, drawn = attention_pair(key, 307)
    weight = drawn
    return weight.astype(jnp.bfloat16)


def normal_values(key, dims, spread, bound, held_as=jnp.bfloat16):
    entries = jax.random.normal(key, dims, jnp.float32) * spread
    return jnp.minimum(jnp.maximum(entries, -bound), bound).astype(held_as)


def setup_inputs(seed: int = 0) -> dict:
    key_list = jax.random.split(jax.random.key(seed), 10)
    return {
        "alignment": draw_alignment(jax.random.fold_in(key_list[9], 71), 0),
        "row_query": draw_row_query(jax.random.fold_in(key_list[9], 71), 0),
        "row_key": draw_row_key(jax.random.fold_in(key_list[9], 71), 0),
        "row_value": normal_values(key_list[3], (D, INNER), D ** -0.5, 0.375),
        "row_output": normal_values(key_list[4], (INNER, D), INNER ** -0.5, 0.5),
        "column_query": draw_column_query(jax.random.fold_in(key_list[9], 71), 0),
        "column_key": draw_column_key(jax.random.fold_in(key_list[9], 71), 0),
        "column_value": normal_values(key_list[7], (D, INNER), D ** -0.5, 0.375),
        "column_output": normal_values(key_list[8], (INNER, D), INNER ** -0.5, 0.5),
    }


def layer_norm(field):
    values = field.astype(jnp.float32)
    mean = lax.optimization_barrier(jnp.mean(values, axis=-1, keepdims=True))
    centred = values - mean
    variance = lax.optimization_barrier(jnp.mean(centred * centred, axis=-1, keepdims=True))
    return (centred * jax.lax.rsqrt(variance + 1e-05)).astype(jnp.bfloat16)

def project(field, weight):
    return jnp.dot(field, weight, preferred_element_type=jnp.float32)

def reference(alignment, row_query, row_key, row_value, row_output, column_query, column_key, column_value, column_output):
    normed = layer_norm(alignment)
    shape4 = (SEQS, COLUMNS, HEADS, HEAD_DIM)
    queries = project(normed, row_query).astype(jnp.bfloat16).astype(jnp.float32).reshape(shape4)
    keys = project(normed, row_key).astype(jnp.bfloat16).astype(jnp.float32).reshape(shape4)
    values = project(normed, row_value).astype(jnp.bfloat16).astype(jnp.float32).reshape(shape4)
    scale = float(HEAD_DIM * SEQS) ** (-0.5)
    logits = jnp.einsum('sihd,sjhd->hij', queries, keys) * scale
    probs = jax.nn.softmax(logits, axis=-1).astype(jnp.bfloat16).astype(jnp.float32)
    context = jnp.einsum('hij,sjhd->sihd', probs, values).reshape(SEQS, COLUMNS, INNER).astype(jnp.bfloat16)
    row_update = project(context, row_output).astype(jnp.bfloat16)
    middle = (alignment.astype(jnp.float32) + row_update.astype(jnp.float32)).astype(jnp.bfloat16)
    column_normed = layer_norm(middle)
    column_queries = project(column_normed, column_query).astype(jnp.bfloat16).astype(jnp.float32).reshape(shape4)
    column_keys = project(column_normed, column_key).astype(jnp.bfloat16).astype(jnp.float32).reshape(shape4)
    column_values = project(column_normed, column_value).astype(jnp.bfloat16).astype(jnp.float32).reshape(shape4)
    scores = jnp.einsum('schd,tchd->chst', column_queries, column_keys) * float(HEAD_DIM) ** (-0.5)
    column_probs = jax.nn.softmax(scores, axis=-1).astype(jnp.bfloat16).astype(jnp.float32)
    column_context = jnp.einsum('chst,tchd->schd', column_probs, column_values).reshape(SEQS, COLUMNS, INNER).astype(jnp.bfloat16)
    layer_output = (middle.astype(jnp.float32) + project(column_context, column_output)).astype(jnp.bfloat16)
    return (row_update, layer_output)
```

```python
import jax
import jax.numpy as jnp
from jax import lax
from jax.sharding import PartitionSpec as P

HEADS = 4
HEAD_DIM = 32


def layer_norm(field):
    values = field.astype(jnp.float32)
    mean = jnp.mean(values, axis=-1, keepdims=True)
    centred = values - mean
    variance = jnp.mean(centred * centred, axis=-1, keepdims=True)
    return (centred * lax.rsqrt(variance + 1e-05)).astype(jnp.bfloat16)


def project(field, weight):
    return jnp.dot(field, weight, preferred_element_type=jnp.float32)


def gather(block, axis, groups=None, size=None):
    size = lax.axis_size(axis) if size is None else size
    copies = jnp.broadcast_to(block[None], (size,) + block.shape)
    return lax.all_to_all(copies, axis, 0, 0, axis_index_groups=groups)


def gather_columns(block):
    size = lax.axis_size("col")
    if size % 2 or size == 2:
        return gather(block, "col")
    groups = [[i for i in range(size) if i % 2 == parity] for parity in (0, 1)]
    mine = gather(block, "col", groups, size // 2)
    other = lax.ppermute(mine, "col", [(i, i ^ 1) for i in range(size)])
    return jnp.concatenate([mine, other], axis=0)


def column_attend(queries, keys, values):
    seq_rows, columns, inner = queries.shape
    query_heads = queries.reshape(seq_rows, columns, HEADS, HEAD_DIM)
    key_heads = keys.reshape(keys.shape[0], columns, HEADS, HEAD_DIM)
    value_heads = values.reshape(values.shape[0], columns, HEADS, HEAD_DIM)
    scores = jnp.einsum(
        "schd,tchd->chst", query_heads, key_heads, preferred_element_type=jnp.float32
    ) * float(HEAD_DIM) ** (-0.5)
    weights = jax.nn.softmax(scores, axis=-1).astype(jnp.bfloat16)
    context = jnp.einsum(
        "chst,tchd->schd", weights, value_heads, preferred_element_type=jnp.float32
    )
    return context.reshape(seq_rows, columns, inner).astype(jnp.bfloat16)


def on_device(
    alignment,
    row_query,
    row_key,
    row_value,
    row_output,
    column_query,
    column_key,
    column_value,
    column_output,
):
    seq_dev, col_dev, width = alignment.shape
    inner = row_query.shape[1]
    scale = float(HEAD_DIM * seq_dev * lax.axis_size("seq")) ** (-0.5)
    normed = layer_norm(alignment)
    queries = project(normed, row_query).astype(jnp.bfloat16)
    key_value = project(normed, jnp.concatenate([row_key, row_value], axis=1)).astype(jnp.bfloat16)
    query_heads = queries.reshape(seq_dev, col_dev, HEADS, HEAD_DIM)
    every = gather_columns(key_value)
    key_heads = every[..., :inner].reshape(every.shape[0], seq_dev, col_dev, HEADS, HEAD_DIM)
    value_heads = every[..., inner:].reshape(every.shape[0], seq_dev, col_dev, HEADS, HEAD_DIM)
    partial_value = jnp.einsum(
        "sihd,gsjhd->higj", query_heads, key_heads, preferred_element_type=jnp.float32
    )
    shape = partial_value.shape
    partial_value = partial_value.reshape(shape[0], shape[1], -1)
    logits = jnp.sum(gather(partial_value, "seq"), axis=0) * scale
    probs = jax.nn.softmax(logits, axis=-1).astype(jnp.bfloat16).reshape(shape)
    context = jnp.einsum("higj,gsjhd->sihd", probs, value_heads, preferred_element_type=jnp.float32)
    context = context.reshape(seq_dev, col_dev, inner).astype(jnp.bfloat16)
    row_update = project(context, row_output).astype(jnp.bfloat16)
    middle = (alignment.astype(jnp.float32) + row_update.astype(jnp.float32)).astype(jnp.bfloat16)
    column_normed = layer_norm(middle)
    column_queries = project(column_normed, column_query).astype(jnp.bfloat16)
    column_pair = project(column_normed, jnp.concatenate([column_key, column_value], axis=1))
    every = gather(column_pair.astype(jnp.bfloat16), "seq")
    every = every.reshape((-1,) + every.shape[2:])
    column_context = column_attend(column_queries, every[..., :inner], every[..., inner:])
    layer_output = (middle.astype(jnp.float32) + project(column_context, column_output)).astype(
        jnp.bfloat16
    )
    return (row_update, layer_output)


def solution(mesh):
    return jax.shard_map(
        on_device,
        mesh=mesh,
        in_specs=(P("seq", "col", None), P(), P(), P(), P(), P(), P(), P(), P()),
        out_specs=(P("seq", "col", None), P("seq", "col", None)),
        check_vma=False,
    )
```

```python
import jax
import jax.numpy as jnp
from jax import lax
from jax.experimental import pallas as pl
from jax.experimental.pallas import tpu as pltpu
from jax.sharding import PartitionSpec as P

HEADS = 4
HEAD_DIM = 32


def layer_norm(field):
    values = field.astype(jnp.float32)
    mean = jnp.mean(values, axis=-1, keepdims=True)
    centred = values - mean
    variance = jnp.mean(centred * centred, axis=-1, keepdims=True)
    return (centred * lax.rsqrt(variance + 1e-05)).astype(jnp.bfloat16)


def project(field, weight):
    return jnp.dot(field, weight, preferred_element_type=jnp.float32)


def gather(block, axis, groups=None, size=None):
    size = lax.axis_size(axis) if size is None else size
    copies = jnp.broadcast_to(block[None], (size,) + block.shape)
    return lax.all_to_all(copies, axis, 0, 0, axis_index_groups=groups)


def gather_columns(block):
    size = lax.axis_size("col")
    if size % 2 or size == 2:
        return gather(block, "col")
    groups = [[i for i in range(size) if i % 2 == parity] for parity in (0, 1)]
    mine = gather(block, "col", groups, size // 2)
    other = lax.ppermute(mine, "col", [(i, i ^ 1) for i in range(size)])
    return jnp.concatenate([mine, other], axis=0)


def column_attend(queries, keys, values):
    seq_rows, columns, inner = queries.shape
    query_heads = queries.reshape(seq_rows, columns, HEADS, HEAD_DIM)
    key_heads = keys.reshape(keys.shape[0], columns, HEADS, HEAD_DIM)
    value_heads = values.reshape(values.shape[0], columns, HEADS, HEAD_DIM)
    scores = jnp.einsum(
        "schd,tchd->chst", query_heads, key_heads, preferred_element_type=jnp.float32
    ) * float(HEAD_DIM) ** (-0.5)
    weights = jax.nn.softmax(scores, axis=-1).astype(jnp.bfloat16)
    context = jnp.einsum(
        "chst,tchd->schd", weights, value_heads, preferred_element_type=jnp.float32
    )
    return context.reshape(seq_rows, columns, inner).astype(jnp.bfloat16)


def on_device(
    alignment,
    row_query,
    row_key,
    row_value,
    row_output,
    column_query,
    column_key,
    column_value,
    column_output,
):
    seq_dev, col_dev, width = alignment.shape
    inner = row_query.shape[1]
    scale = float(HEAD_DIM * seq_dev * lax.axis_size("seq")) ** (-0.5)
    normed = layer_norm(alignment)
    queries = project(normed, row_query).astype(jnp.bfloat16)
    key_value = project(normed, jnp.concatenate([row_key, row_value], axis=1)).astype(jnp.bfloat16)
    query_heads = queries.reshape(seq_dev, col_dev, HEADS, HEAD_DIM)
    every = gather_columns(key_value)
    key_heads = every[..., :inner].reshape(every.shape[0], seq_dev, col_dev, HEADS, HEAD_DIM)
    value_heads = every[..., inner:].reshape(every.shape[0], seq_dev, col_dev, HEADS, HEAD_DIM)
    partial_value = jnp.einsum(
        "sihd,gsjhd->higj", query_heads, key_heads, preferred_element_type=jnp.float32
    )
    shape = partial_value.shape
    partial_value = partial_value.reshape(shape[0], shape[1], -1)
    logits = jnp.sum(gather(partial_value, "seq"), axis=0) * scale
    probs = jax.nn.softmax(logits, axis=-1).astype(jnp.bfloat16).reshape(shape)
    context = jnp.einsum("higj,gsjhd->sihd", probs, value_heads, preferred_element_type=jnp.float32)
    context = context.reshape(seq_dev, col_dev, inner).astype(jnp.bfloat16)
    row_update = project(context, row_output).astype(jnp.bfloat16)
    middle = (alignment.astype(jnp.float32) + row_update.astype(jnp.float32)).astype(jnp.bfloat16)
    column_normed = layer_norm(middle)
    column_queries = project(column_normed, column_query).astype(jnp.bfloat16)
    column_pair = project(column_normed, jnp.concatenate([column_key, column_value], axis=1))
    every = gather(column_pair.astype(jnp.bfloat16), "seq")
    every = every.reshape((-1,) + every.shape[2:])
    column_context = column_attend(column_queries, every[..., :inner], every[..., inner:])
    layer_output = (middle.astype(jnp.float32) + project(column_context, column_output)).astype(
        jnp.bfloat16
    )
    return (row_update, layer_output)


def norm_rows(values):
    mean = jnp.mean(values, axis=-1, keepdims=True)
    centred = values - mean
    variance = jnp.mean(centred * centred, axis=-1, keepdims=True)
    return (centred * lax.rsqrt(variance + 1e-05)).astype(jnp.bfloat16)


def swap_groups(arrays, group):
    lanes = arrays[0].shape[-1]
    index = lax.broadcasted_iota(jnp.int32, arrays[0].shape, 1) // group
    arrays = list(arrays)
    step = len(arrays) // 2
    while step:
        low = (index // step) % 2 == 0
        for first in range(len(arrays)):
            if (first // step) % 2 == 0:
                one, two = arrays[first], arrays[first + step]
                shift = step * group
                arrays[first] = jnp.where(low, one, pltpu.roll(two, shift, 1))
                arrays[first + step] = jnp.where(low, pltpu.roll(one, lanes - shift, 1), two)
        step //= 2
    return arrays


def contract_last(left, right):
    return lax.dot_general(
        left, right, (((1,), (1,)), ((), ())), preferred_element_type=jnp.float32
    )


def project_kernel(field_ref, key_ref, value_ref, query_ref, out_ref):
    seq_dev, col_dev, width = field_ref.shape
    heads, chips, cores = out_ref.shape[:3]
    normed = norm_rows(field_ref[...].astype(jnp.float32).reshape(seq_dev * col_dev, width))
    for kind, weight_ref in enumerate((key_ref, value_ref, query_ref)):
        rows = project(normed, weight_ref[...])
        for core in range(cores):
            first = core * heads
            tiles = [
                rows[(first + place) * col_dev : (first + place + 1) * col_dev]
                for place in range(heads)
            ]
            for head, tile in enumerate(swap_groups(tiles, HEAD_DIM)):
                tile = tile.astype(jnp.bfloat16)
                for chip in range(chips):
                    out_ref[head, chip, core, kind] = tile


def attend_kernel(scale, mine_ref, other_ref, field_ref, out_ref):
    column = lax.axis_index("col")
    core = lax.rem(column, 2)
    seq, col, _, col_dev, lanes = mine_ref.shape
    seq_dev = field_ref.shape[0]
    logits = jnp.zeros((col_dev, col * col_dev), jnp.float32)
    for ref in (mine_ref, other_ref):
        for source in range(seq):
            keys = ref[source, :, 0].reshape(col * col_dev, lanes)
            logits += contract_last(ref[source, column, 2], keys)
    logits = logits * scale
    weights = jnp.exp(logits - jnp.max(logits, axis=-1, keepdims=True))
    probs = (weights / jnp.sum(weights, axis=-1, keepdims=True)).astype(jnp.bfloat16)
    for ref, half in ((mine_ref, core), (other_ref, 1 - core)):
        for source in range(seq):
            values = ref[source, :, 1].reshape(col * col_dev, lanes)
            context = project(probs, values).astype(jnp.bfloat16)
            for copy in range(seq):
                out_ref[copy, half * seq + source] = context
    start = 2 * seq
    for part in range(field_ref.shape[2] // lanes):
        field = field_ref[:, :, part * lanes : (part + 1) * lanes]
        for copy in range(seq):
            out_ref[copy, start : start + seq_dev] = field
        start += seq_dev


def finish_kernel(
    parts_ref,
    row_output_ref,
    query_ref,
    key_ref,
    value_ref,
    output_ref,
    update_ref,
    layer_ref,
    updates,
    middles,
    normals,
    queries,
    keys,
    values,
    contexts,
):
    own = lax.axis_index("seq")
    seq, tiles, col_dev, lanes = parts_ref.shape
    seq_dev, _, width = update_ref.shape
    rows = seq_dev * col_dev
    seqs = seq * seq_dev
    for source in range(seq):
        context = []
        for half in range(seq_dev // HEADS):
            heads = [
                parts_ref[head, half * seq + source].astype(jnp.float32) for head in range(HEADS)
            ]
            context += swap_groups(heads, HEAD_DIM)
        context = jnp.concatenate(context, axis=0).astype(jnp.bfloat16)
        update = project(context, row_output_ref[...]).astype(jnp.bfloat16)
        start = seq * seq_dev // HEADS
        field = jnp.concatenate(
            [
                parts_ref[source, first : first + seq_dev].reshape(rows, lanes)
                for first in range(start, tiles, seq_dev)
            ],
            axis=1,
        )
        middle = (field.astype(jnp.float32) + update.astype(jnp.float32)).astype(jnp.bfloat16)
        normal = norm_rows(middle.astype(jnp.float32))
        place = slice(source * rows, (source + 1) * rows)
        updates[place, :] = update
        middles[place, :] = middle
        normals[place, :] = normal
        keys[place, :] = project(normal, key_ref[...]).astype(jnp.bfloat16).astype(jnp.float32)
        values[place, :] = project(normal, value_ref[...]).astype(jnp.bfloat16).astype(jnp.float32)
    mine = pl.ds(pl.multiple_of(own * rows, rows), rows)
    update_ref[...] = updates[mine, :].reshape(update_ref.shape)
    queries[...] = (
        project(normals[mine, :], query_ref[...]).astype(jnp.bfloat16).astype(jnp.float32)
    )
    group = lanes // seqs
    head_of = lax.broadcasted_iota(jnp.int32, (seq_dev, lanes), 1) // HEAD_DIM
    size = group * seqs
    row_column = lax.broadcasted_iota(jnp.int32, (group * HEADS * seq_dev, size), 0) // (
        HEADS * seq_dev
    )
    same = row_column == lax.broadcasted_iota(jnp.int32, row_column.shape, 1) // seqs
    for first in range(0, col_dev, group):
        query, key, value = [], [], []
        for column in range(first, first + group):
            row = queries[pl.ds(column, seq_dev, stride=col_dev), :]
            query += [jnp.where(head_of == head, row, 0.0) for head in range(HEADS)]
            key.append(keys[pl.ds(column, seqs, stride=col_dev), :])
            value.append(values[pl.ds(column, seqs, stride=col_dev), :])
        query, key, value = (
            jnp.concatenate(part, axis=0).astype(jnp.bfloat16) for part in (query, key, value)
        )
        scores = jnp.where(
            same, contract_last(query, key) * float(HEAD_DIM) ** (-0.5), -jnp.inf
        )
        weights = jnp.exp(scores - jnp.max(scores, axis=-1, keepdims=True))
        probs = (weights / jnp.sum(weights, axis=-1, keepdims=True)).astype(jnp.bfloat16)
        context = project(probs, value)
        for place in range(group):
            total = jnp.zeros((seq_dev, lanes), jnp.float32)
            for head in range(HEADS):
                at = (place * HEADS + head) * seq_dev
                total = jnp.where(head_of == head, context[at : at + seq_dev], total)
            contexts[pl.ds(first + place, seq_dev, stride=col_dev), :] = total
    layer = middles[mine, :].astype(jnp.float32) + project(
        contexts[...].astype(jnp.bfloat16), output_ref[...]
    )
    layer_ref[...] = layer.astype(jnp.bfloat16).reshape(layer_ref.shape)


def by_head(
    alignment,
    row_query,
    row_key,
    row_value,
    row_output,
    column_query,
    column_key,
    column_value,
    column_output,
):
    seq_dev, col_dev, width = alignment.shape
    inner = row_query.shape[1]
    seq, col = lax.axis_size("seq"), lax.axis_size("col")
    scale = float(HEAD_DIM * seq_dev * seq) ** (-0.5)
    bf16 = jnp.bfloat16
    vmem = pl.BlockSpec(memory_space=pltpu.VMEM)
    blocks = pl.pallas_call(
        project_kernel,
        out_shape=jax.ShapeDtypeStruct((seq, col // 2, 2, 3, col_dev, inner), bf16),
        in_specs=[vmem] * 4,
        out_specs=vmem,
        compiler_params=pltpu.CompilerParams(vmem_limit_bytes=8 << 20),
        name="project",
    )(alignment, row_key, row_value, row_query)
    mine = lax.all_to_all(
        blocks.reshape(seq * col, 3, col_dev, inner), ("seq", "col"), 0, 0
    )
    other = lax.ppermute(mine, "col", [(i, i ^ 1) for i in range(col)])
    shape = (seq, col, 3, col_dev, inner)
    tiles = seq_dev // HEADS * seq + width // inner * seq_dev
    parts = pl.pallas_call(
        lambda *refs: attend_kernel(scale, *refs),
        out_shape=jax.ShapeDtypeStruct((seq, tiles, col_dev, inner), bf16),
        in_specs=[vmem] * 3,
        out_specs=vmem,
        compiler_params=pltpu.CompilerParams(vmem_limit_bytes=8 << 20),
        name="attend",
    )(mine.reshape(shape), other.reshape(shape), alignment)
    parts = lax.all_to_all(parts, "seq", 0, 0)
    total = seq * seq_dev * col_dev
    local = seq_dev * col_dev
    like = jax.ShapeDtypeStruct(alignment.shape, bf16)
    f32 = jnp.float32
    return pl.pallas_call(
        finish_kernel,
        out_shape=(like, like),
        in_specs=[vmem] * 6,
        out_specs=(vmem, vmem),
        scratch_shapes=[
            pltpu.VMEM((total, width), bf16),
            pltpu.VMEM((total, width), bf16),
            pltpu.VMEM((total, width), bf16),
            pltpu.VMEM((local, inner), f32),
            pltpu.VMEM((total, inner), f32),
            pltpu.VMEM((total, inner), f32),
            pltpu.VMEM((local, inner), f32),
        ],
        compiler_params=pltpu.CompilerParams(vmem_limit_bytes=8 << 20),
        name="finish",
    )(parts, row_output, column_query, column_key, column_value, column_output)


def suits_by_head(seq, col, seq_dev, col_dev, width, inner):
    return (
        seq == HEADS
        and col % 2 == 0
        and seq_dev == 2 * HEADS
        and col_dev % 16 == 0
        and inner == HEADS * HEAD_DIM
        and inner == 128
        and width % inner == 0
        and inner % (seq * seq_dev) == 0
        and col_dev % (inner // (seq * seq_dev)) == 0
        and seq * seq_dev * col_dev <= 1024
        and col * col_dev <= 512
    )


def solution(mesh):
    def choose(*args):
        seq_dev, col_dev, width = args[0].shape
        sizes = (mesh.shape["seq"], mesh.shape["col"], seq_dev, col_dev, width, args[1].shape[1])
        return (by_head if suits_by_head(*sizes) else on_device)(*args)

    return jax.shard_map(
        choose,
        mesh=mesh,
        in_specs=(P("seq", "col", None), P(), P(), P(), P(), P(), P(), P(), P()),
        out_specs=(P("seq", "col", None), P("seq", "col", None)),
        check_vma=False,
    )
```

```python
import jax
import jax.numpy as jnp
from jax import lax
from jax.experimental import pallas as pl
from jax.experimental.pallas import tpu as pltpu
from jax.sharding import PartitionSpec as P

HEADS = 4
HEAD_DIM = 32


def layer_norm(field):
    values = field.astype(jnp.float32)
    mean = jnp.mean(values, axis=-1, keepdims=True)
    centred = values - mean
    variance = jnp.mean(centred * centred, axis=-1, keepdims=True)
    return (centred * lax.rsqrt(variance + 1e-05)).astype(jnp.bfloat16)


def project(field, weight):
    return jnp.dot(field, weight, preferred_element_type=jnp.float32)


def gather(block, axis, groups=None, size=None):
    size = lax.axis_size(axis) if size is None else size
    copies = jnp.broadcast_to(block[None], (size,) + block.shape)
    return lax.all_to_all(copies, axis, 0, 0, axis_index_groups=groups)


def gather_columns(block):
    size = lax.axis_size("col")
    if size % 2 or size == 2:
        return gather(block, "col")
    groups = [[i for i in range(size) if i % 2 == parity] for parity in (0, 1)]
    mine = gather(block, "col", groups, size // 2)
    other = lax.ppermute(mine, "col", [(i, i ^ 1) for i in range(size)])
    return jnp.concatenate([mine, other], axis=0)


def column_attend(queries, keys, values):
    seq_rows, columns, inner = queries.shape
    query_heads = queries.reshape(seq_rows, columns, HEADS, HEAD_DIM)
    key_heads = keys.reshape(keys.shape[0], columns, HEADS, HEAD_DIM)
    value_heads = values.reshape(values.shape[0], columns, HEADS, HEAD_DIM)
    scores = jnp.einsum(
        "schd,tchd->chst", query_heads, key_heads, preferred_element_type=jnp.float32
    ) * float(HEAD_DIM) ** (-0.5)
    weights = jax.nn.softmax(scores, axis=-1).astype(jnp.bfloat16)
    context = jnp.einsum(
        "chst,tchd->schd", weights, value_heads, preferred_element_type=jnp.float32
    )
    return context.reshape(seq_rows, columns, inner).astype(jnp.bfloat16)


def on_device(
    alignment,
    row_query,
    row_key,
    row_value,
    row_output,
    column_query,
    column_key,
    column_value,
    column_output,
):
    seq_dev, col_dev, width = alignment.shape
    inner = row_query.shape[1]
    scale = float(HEAD_DIM * seq_dev * lax.axis_size("seq")) ** (-0.5)
    normed = layer_norm(alignment)
    queries = project(normed, row_query).astype(jnp.bfloat16)
    key_value = project(normed, jnp.concatenate([row_key, row_value], axis=1)).astype(jnp.bfloat16)
    query_heads = queries.reshape(seq_dev, col_dev, HEADS, HEAD_DIM)
    every = gather_columns(key_value)
    key_heads = every[..., :inner].reshape(every.shape[0], seq_dev, col_dev, HEADS, HEAD_DIM)
    value_heads = every[..., inner:].reshape(every.shape[0], seq_dev, col_dev, HEADS, HEAD_DIM)
    partial_value = jnp.einsum(
        "sihd,gsjhd->higj", query_heads, key_heads, preferred_element_type=jnp.float32
    )
    shape = partial_value.shape
    partial_value = partial_value.reshape(shape[0], shape[1], -1)
    logits = jnp.sum(gather(partial_value, "seq"), axis=0) * scale
    probs = jax.nn.softmax(logits, axis=-1).astype(jnp.bfloat16).reshape(shape)
    context = jnp.einsum("higj,gsjhd->sihd", probs, value_heads, preferred_element_type=jnp.float32)
    context = context.reshape(seq_dev, col_dev, inner).astype(jnp.bfloat16)
    row_update = project(context, row_output).astype(jnp.bfloat16)
    middle = (alignment.astype(jnp.float32) + row_update.astype(jnp.float32)).astype(jnp.bfloat16)
    column_normed = layer_norm(middle)
    column_queries = project(column_normed, column_query).astype(jnp.bfloat16)
    column_pair = project(column_normed, jnp.concatenate([column_key, column_value], axis=1))
    every = gather(column_pair.astype(jnp.bfloat16), "seq")
    every = every.reshape((-1,) + every.shape[2:])
    column_context = column_attend(column_queries, every[..., :inner], every[..., inner:])
    layer_output = (middle.astype(jnp.float32) + project(column_context, column_output)).astype(
        jnp.bfloat16
    )
    return (row_update, layer_output)


def norm_rows(values):
    mean = jnp.mean(values, axis=-1, keepdims=True)
    centred = values - mean
    variance = jnp.mean(centred * centred, axis=-1, keepdims=True)
    return (centred * lax.rsqrt(variance + 1e-05)).astype(jnp.bfloat16)


def swap_groups(arrays, group):
    lanes = arrays[0].shape[-1]
    index = lax.broadcasted_iota(jnp.int32, arrays[0].shape, 1) // group
    arrays = list(arrays)
    step = len(arrays) // 2
    while step:
        low = (index // step) % 2 == 0
        for first in range(len(arrays)):
            if (first // step) % 2 == 0:
                one, two = arrays[first], arrays[first + step]
                shift = step * group
                arrays[first] = jnp.where(low, one, pltpu.roll(two, shift, 1))
                arrays[first + step] = jnp.where(low, pltpu.roll(one, lanes - shift, 1), two)
        step //= 2
    return arrays


def contract_last(left, right):
    return lax.dot_general(
        left, right, (((1,), (1,)), ((), ())), preferred_element_type=jnp.float32
    )


def project_kernel(*refs):
    sources, out_ref, held, sems = refs[:4], refs[4], refs[5:9], refs[9]
    copies = [
        pltpu.make_async_copy(source, ref, sems.at[place])
        for place, (source, ref) in enumerate(zip(sources, held))
    ]
    for copy in copies:
        copy.start()
    field_ref, key_ref, value_ref, query_ref = held
    seq_dev, col_dev, width = field_ref.shape
    heads, chips, cores = out_ref.shape[:3]
    copies[0].wait()
    normed = norm_rows(field_ref[...].astype(jnp.float32).reshape(seq_dev * col_dev, width))
    for kind, weight_ref in enumerate((key_ref, value_ref, query_ref)):
        copies[kind + 1].wait()
        rows = project(normed, weight_ref[...])
        for core in range(cores):
            first = core * heads
            tiles = [
                rows[(first + place) * col_dev : (first + place + 1) * col_dev]
                for place in range(heads)
            ]
            for head, tile in enumerate(swap_groups(tiles, HEAD_DIM)):
                tile = tile.astype(jnp.bfloat16)
                for chip in range(chips):
                    out_ref[head, chip, core, kind] = tile


def attend_kernel(scale, mine_ref, other_ref, field_ref, out_ref):
    column = lax.axis_index("col")
    core = lax.rem(column, 2)
    seq, col, _, col_dev, lanes = mine_ref.shape
    seq_dev = field_ref.shape[0]
    logits = jnp.zeros((col_dev, col * col_dev), jnp.float32)
    for ref in (mine_ref, other_ref):
        for source in range(seq):
            keys = ref[source, :, 0].reshape(col * col_dev, lanes)
            logits += contract_last(ref[source, column, 2], keys)
    logits = logits * scale
    weights = jnp.exp(logits - jnp.max(logits, axis=-1, keepdims=True))
    probs = (weights / jnp.sum(weights, axis=-1, keepdims=True)).astype(jnp.bfloat16)
    for ref, half in ((mine_ref, core), (other_ref, 1 - core)):
        for source in range(seq):
            values = ref[source, :, 1].reshape(col * col_dev, lanes)
            context = project(probs, values).astype(jnp.bfloat16)
            for copy in range(seq):
                out_ref[copy, half * seq + source] = context
    start = 2 * seq
    for part in range(field_ref.shape[2] // lanes):
        field = field_ref[:, :, part * lanes : (part + 1) * lanes]
        for copy in range(seq):
            out_ref[copy, start : start + seq_dev] = field
        start += seq_dev


def finish_kernel(
    parts_ref,
    row_output_ref,
    query_ref,
    key_ref,
    value_ref,
    output_ref,
    update_ref,
    layer_ref,
    updates,
    middles,
    normals,
    queries,
    keys,
    values,
    contexts,
):
    own = lax.axis_index("seq")
    seq, tiles, col_dev, lanes = parts_ref.shape
    seq_dev, _, width = update_ref.shape
    rows = seq_dev * col_dev
    seqs = seq * seq_dev
    for source in range(seq):
        context = []
        for half in range(seq_dev // HEADS):
            heads = [
                parts_ref[head, half * seq + source].astype(jnp.float32) for head in range(HEADS)
            ]
            context += swap_groups(heads, HEAD_DIM)
        context = jnp.concatenate(context, axis=0).astype(jnp.bfloat16)
        update = project(context, row_output_ref[...]).astype(jnp.bfloat16)
        start = seq * seq_dev // HEADS
        field = jnp.concatenate(
            [
                parts_ref[source, first : first + seq_dev].reshape(rows, lanes)
                for first in range(start, tiles, seq_dev)
            ],
            axis=1,
        )
        middle = (field.astype(jnp.float32) + update.astype(jnp.float32)).astype(jnp.bfloat16)
        normal = norm_rows(middle.astype(jnp.float32))
        place = slice(source * rows, (source + 1) * rows)
        updates[place, :] = update
        middles[place, :] = middle
        normals[place, :] = normal
        keys[place, :] = project(normal, key_ref[...]).astype(jnp.bfloat16).astype(jnp.float32)
        values[place, :] = project(normal, value_ref[...]).astype(jnp.bfloat16).astype(jnp.float32)
    mine = pl.ds(pl.multiple_of(own * rows, rows), rows)
    update_ref[...] = updates[mine, :].reshape(update_ref.shape)
    queries[...] = (
        project(normals[mine, :], query_ref[...]).astype(jnp.bfloat16).astype(jnp.float32)
    )
    group = lanes // seqs
    head_of = lax.broadcasted_iota(jnp.int32, (seq_dev, lanes), 1) // HEAD_DIM
    size = group * seqs
    row_column = lax.broadcasted_iota(jnp.int32, (group * HEADS * seq_dev, size), 0) // (
        HEADS * seq_dev
    )
    same = row_column == lax.broadcasted_iota(jnp.int32, row_column.shape, 1) // seqs
    for first in range(0, col_dev, group):
        query, key, value = [], [], []
        for column in range(first, first + group):
            row = queries[pl.ds(column, seq_dev, stride=col_dev), :]
            query += [jnp.where(head_of == head, row, 0.0) for head in range(HEADS)]
            key.append(keys[pl.ds(column, seqs, stride=col_dev), :])
            value.append(values[pl.ds(column, seqs, stride=col_dev), :])
        query, key, value = (
            jnp.concatenate(part, axis=0).astype(jnp.bfloat16) for part in (query, key, value)
        )
        scores = jnp.where(
            same, contract_last(query, key) * float(HEAD_DIM) ** (-0.5), -jnp.inf
        )
        weights = jnp.exp(scores - jnp.max(scores, axis=-1, keepdims=True))
        probs = (weights / jnp.sum(weights, axis=-1, keepdims=True)).astype(jnp.bfloat16)
        context = project(probs, value)
        for place in range(group):
            total = jnp.zeros((seq_dev, lanes), jnp.float32)
            for head in range(HEADS):
                at = (place * HEADS + head) * seq_dev
                total = jnp.where(head_of == head, context[at : at + seq_dev], total)
            contexts[pl.ds(first + place, seq_dev, stride=col_dev), :] = total
    layer = middles[mine, :].astype(jnp.float32) + project(
        contexts[...].astype(jnp.bfloat16), output_ref[...]
    )
    layer_ref[...] = layer.astype(jnp.bfloat16).reshape(layer_ref.shape)


def by_head(
    alignment,
    row_query,
    row_key,
    row_value,
    row_output,
    column_query,
    column_key,
    column_value,
    column_output,
):
    seq_dev, col_dev, width = alignment.shape
    inner = row_query.shape[1]
    seq, col = lax.axis_size("seq"), lax.axis_size("col")
    scale = float(HEAD_DIM * seq_dev * seq) ** (-0.5)
    bf16 = jnp.bfloat16
    vmem = pl.BlockSpec(memory_space=pltpu.VMEM)
    sources = (alignment, row_key, row_value, row_query)
    blocks = pl.pallas_call(
        project_kernel,
        out_shape=jax.ShapeDtypeStruct((seq, col // 2, 2, 3, col_dev, inner), bf16),
        in_specs=[pl.BlockSpec(memory_space=pltpu.HBM)] * 4,
        out_specs=vmem,
        scratch_shapes=[pltpu.VMEM(alignment.shape, bf16)]
        + [pltpu.VMEM(row_key.shape, bf16)] * 3
        + [pltpu.SemaphoreType.DMA((4,))],
        compiler_params=pltpu.CompilerParams(vmem_limit_bytes=8 << 20),
        name="project",
    )(*(pltpu.with_memory_space_constraint(x, pltpu.HBM) for x in sources))
    mine = lax.all_to_all(
        blocks.reshape(seq * col, 3, col_dev, inner), ("seq", "col"), 0, 0
    )
    other = lax.ppermute(mine, "col", [(i, i ^ 1) for i in range(col)])
    shape = (seq, col, 3, col_dev, inner)
    tiles = seq_dev // HEADS * seq + width // inner * seq_dev
    parts = pl.pallas_call(
        lambda *refs: attend_kernel(scale, *refs),
        out_shape=jax.ShapeDtypeStruct((seq, tiles, col_dev, inner), bf16),
        in_specs=[vmem] * 3,
        out_specs=vmem,
        compiler_params=pltpu.CompilerParams(vmem_limit_bytes=8 << 20),
        name="attend",
    )(mine.reshape(shape), other.reshape(shape), alignment)
    parts = lax.all_to_all(parts, "seq", 0, 0)
    total = seq * seq_dev * col_dev
    local = seq_dev * col_dev
    like = jax.ShapeDtypeStruct(alignment.shape, bf16)
    f32 = jnp.float32
    return pl.pallas_call(
        finish_kernel,
        out_shape=(like, like),
        in_specs=[vmem] * 6,
        out_specs=(vmem, vmem),
        scratch_shapes=[
            pltpu.VMEM((total, width), bf16),
            pltpu.VMEM((total, width), bf16),
            pltpu.VMEM((total, width), bf16),
            pltpu.VMEM((local, inner), f32),
            pltpu.VMEM((total, inner), f32),
            pltpu.VMEM((total, inner), f32),
            pltpu.VMEM((local, inner), f32),
        ],
        compiler_params=pltpu.CompilerParams(vmem_limit_bytes=8 << 20),
        name="finish",
    )(parts, row_output, column_query, column_key, column_value, column_output)


def suits_by_head(seq, col, seq_dev, col_dev, width, inner):
    return (
        seq == HEADS
        and col % 2 == 0
        and seq_dev == 2 * HEADS
        and col_dev % 16 == 0
        and inner == HEADS * HEAD_DIM
        and inner == 128
        and width % inner == 0
        and inner % (seq * seq_dev) == 0
        and col_dev % (inner // (seq * seq_dev)) == 0
        and seq * seq_dev * col_dev <= 1024
        and col * col_dev <= 512
    )


def solution(mesh):
    def choose(*args):
        seq_dev, col_dev, width = args[0].shape
        sizes = (mesh.shape["seq"], mesh.shape["col"], seq_dev, col_dev, width, args[1].shape[1])
        return (by_head if suits_by_head(*sizes) else on_device)(*args)

    return jax.shard_map(
        choose,
        mesh=mesh,
        in_specs=(P("seq", "col", None), P(), P(), P(), P(), P(), P(), P(), P()),
        out_specs=(P("seq", "col", None), P("seq", "col", None)),
        check_vma=False,
    )
```

```python
import functools

import jax
import jax.numpy as jnp
from jax import lax
from jax.experimental import pallas as pl
from jax.experimental.pallas import tpu as pltpu
from jax.sharding import PartitionSpec as P


HEADS = 4
HEAD_DIM = 32


def layer_norm(field):
    values = field.astype(jnp.float32)
    mean = jnp.mean(values, axis=-1, keepdims=True)
    centred = values - mean
    variance = jnp.mean(centred * centred, axis=-1, keepdims=True)
    return (centred * lax.rsqrt(variance + 1e-05)).astype(jnp.bfloat16)


def project(field, weight):
    return jnp.dot(field, weight, preferred_element_type=jnp.float32)


def gather(block, axis, groups=None, size=None):
    size = lax.axis_size(axis) if size is None else size
    copies = jnp.broadcast_to(block[None], (size,) + block.shape)
    return lax.all_to_all(copies, axis, 0, 0, axis_index_groups=groups)


def gather_columns(block):
    size = lax.axis_size("col")
    if size % 2 or size == 2:
        return gather(block, "col")
    groups = [[i for i in range(size) if i % 2 == parity] for parity in (0, 1)]
    mine = gather(block, "col", groups, size // 2)
    other = lax.ppermute(mine, "col", [(i, i ^ 1) for i in range(size)])
    return jnp.concatenate([mine, other], axis=0)


def column_attend(queries, keys, values):
    seq_rows, columns, inner = queries.shape
    query_heads = queries.reshape(seq_rows, columns, HEADS, HEAD_DIM)
    key_heads = keys.reshape(keys.shape[0], columns, HEADS, HEAD_DIM)
    value_heads = values.reshape(values.shape[0], columns, HEADS, HEAD_DIM)
    scores = jnp.einsum(
        "schd,tchd->chst", query_heads, key_heads, preferred_element_type=jnp.float32
    ) * float(HEAD_DIM) ** (-0.5)
    weights = jax.nn.softmax(scores, axis=-1).astype(jnp.bfloat16)
    context = jnp.einsum(
        "chst,tchd->schd", weights, value_heads, preferred_element_type=jnp.float32
    )
    return context.reshape(seq_rows, columns, inner).astype(jnp.bfloat16)


def on_device(
    alignment,
    row_query,
    row_key,
    row_value,
    row_output,
    column_query,
    column_key,
    column_value,
    column_output,
):
    seq_dev, col_dev, _ = alignment.shape
    inner = row_query.shape[1]
    scale = float(HEAD_DIM * seq_dev * lax.axis_size("seq")) ** (-0.5)
    normed = layer_norm(alignment)
    queries = project(normed, row_query).astype(jnp.bfloat16)
    key_value = project(normed, jnp.concatenate([row_key, row_value], axis=1)).astype(jnp.bfloat16)
    query_heads = queries.reshape(seq_dev, col_dev, HEADS, HEAD_DIM)
    every = gather_columns(key_value)
    key_heads = every[..., :inner].reshape(every.shape[0], seq_dev, col_dev, HEADS, HEAD_DIM)
    value_heads = every[..., inner:].reshape(every.shape[0], seq_dev, col_dev, HEADS, HEAD_DIM)
    partial_value = jnp.einsum(
        "sihd,gsjhd->higj", query_heads, key_heads, preferred_element_type=jnp.float32
    )
    shape = partial_value.shape
    partial_value = partial_value.reshape(shape[0], shape[1], -1)
    logits = jnp.sum(gather(partial_value, "seq"), axis=0) * scale
    probs = jax.nn.softmax(logits, axis=-1).astype(jnp.bfloat16).reshape(shape)
    context = jnp.einsum("higj,gsjhd->sihd", probs, value_heads, preferred_element_type=jnp.float32)
    context = context.reshape(seq_dev, col_dev, inner).astype(jnp.bfloat16)
    row_update = project(context, row_output).astype(jnp.bfloat16)
    middle = (alignment.astype(jnp.float32) + row_update.astype(jnp.float32)).astype(jnp.bfloat16)
    column_normed = layer_norm(middle)
    column_queries = project(column_normed, column_query).astype(jnp.bfloat16)
    column_pair = project(column_normed, jnp.concatenate([column_key, column_value], axis=1))
    every = gather(column_pair.astype(jnp.bfloat16), "seq")
    every = every.reshape((-1,) + every.shape[2:])
    column_context = column_attend(column_queries, every[..., :inner], every[..., inner:])
    layer_output = (middle.astype(jnp.float32) + project(column_context, column_output)).astype(
        jnp.bfloat16
    )
    return (row_update, layer_output)


def norm_rows(values):
    mean = jnp.mean(values, axis=-1, keepdims=True)
    centred = values - mean
    variance = jnp.mean(centred * centred, axis=-1, keepdims=True)
    return (centred * lax.rsqrt(variance + 1e-05)).astype(jnp.bfloat16)


def swap_groups(arrays, group):
    lanes = arrays[0].shape[-1]
    index = lax.broadcasted_iota(jnp.int32, arrays[0].shape, 1) // group
    arrays = list(arrays)
    step = len(arrays) // 2
    while step:
        low = (index // step) % 2 == 0
        for first in range(len(arrays)):
            if (first // step) % 2 == 0:
                one, two = arrays[first], arrays[first + step]
                shift = step * group
                arrays[first] = jnp.where(low, one, pltpu.roll(two, shift, 1))
                arrays[first + step] = jnp.where(low, pltpu.roll(one, lanes - shift, 1), two)
        step //= 2
    return arrays


def contract_last(left, right):
    return lax.dot_general(
        left, right, (((1,), (1,)), ((), ())), preferred_element_type=jnp.float32
    )


def project_kernel(*refs):
    sources, out_ref, held, sems = refs[:3], refs[3], refs[4:7], refs[7]
    copies = [
        pltpu.make_async_copy(source, ref, sems.at[place])
        for place, (source, ref) in enumerate(zip(sources, held))
    ]
    for copy in copies:
        copy.start()
    field_ref, key_ref, value_ref = held
    seq_dev, col_dev, width = field_ref.shape
    heads, chips, cores = out_ref.shape[:3]
    copies[0].wait()
    normed = norm_rows(field_ref[...].astype(jnp.float32).reshape(seq_dev * col_dev, width))
    for kind, weight_ref in enumerate((key_ref, value_ref)):
        copies[kind + 1].wait()
        rows = project(normed, weight_ref[...])
        for core in range(cores):
            first = core * heads
            tiles = [
                rows[(first + place) * col_dev : (first + place + 1) * col_dev]
                for place in range(heads)
            ]
            for head, tile in enumerate(swap_groups(tiles, HEAD_DIM)):
                tile = tile.astype(jnp.bfloat16)
                for chip in range(chips):
                    out_ref[head, chip, core, kind] = tile


def query_kernel(*refs):
    fields, (weight_ref, mine_ref, query_ref, logits_ref) = refs[:-4], refs[-4:]
    own, half = lax.axis_index("seq"), lax.rem(lax.axis_index("col"), 2)
    seq_dev, col_dev, width = fields[0].shape
    seq, col, _, _, lanes = mine_ref.shape
    group = lax.broadcasted_iota(jnp.int32, weight_ref.shape, 1) // HEAD_DIM
    weight = weight_ref[...].astype(jnp.float32)
    spread = []
    for place in range(HEADS):
        shift = lax.rem((place + HEADS - own) * HEAD_DIM, lanes)
        spread.append(jnp.where(group == place, pltpu.roll(weight, shift, 1), 0.0))
    spread = jnp.concatenate(spread, axis=0).astype(jnp.bfloat16)
    normed = []
    for field_ref in fields:
        rows = norm_rows(field_ref[...].astype(jnp.float32).reshape(seq_dev * col_dev, width))
        for first in range(0, seq_dev, HEADS):
            normed.append(
                jnp.concatenate(
                    [
                        rows[place * col_dev : (place + 1) * col_dev]
                        for place in range(first, first + HEADS)
                    ],
                    axis=1,
                )
            )
    queries = project(jnp.concatenate(normed, axis=0), spread).astype(jnp.bfloat16)
    halves = seq_dev // HEADS
    for place in range(seq):
        for part in range(halves):
            start = (place * halves + part) * col_dev
            query_ref[part, own ^ place] = queries[start : start + col_dev]
    logits = jnp.zeros(logits_ref.shape, jnp.float32)
    for source in range(seq):
        keys = mine_ref[source, :, 0].reshape(col * col_dev, lanes)
        logits += contract_last(query_ref[half, source], keys)
    logits_ref[...] = logits


def attend_kernel(scale, mine_ref, other_ref, query_ref, logits_ref, out_ref):
    half = lax.rem(lax.axis_index("col"), 2)
    seq, col, _, col_dev, lanes = mine_ref.shape
    logits = logits_ref[...]
    for source in range(seq):
        keys = other_ref[source, :, 0].reshape(col * col_dev, lanes)
        logits += contract_last(query_ref[1 - half, source], keys)
    logits = logits * scale
    weights = jnp.exp(logits - jnp.max(logits, axis=-1, keepdims=True))
    probs = (weights / jnp.sum(weights, axis=-1, keepdims=True)).astype(jnp.bfloat16)
    for ref, part in ((mine_ref, half), (other_ref, 1 - half)):
        for source in range(seq):
            values = ref[source, :, 1].reshape(col * col_dev, lanes)
            context = project(probs, values).astype(jnp.bfloat16)
            for copy in range(seq):
                out_ref[copy, part * seq + source] = context


def finish_kernel(*refs):
    fields, refs = refs[:-12], refs[-12:]
    (parts_ref, row_output_ref, query_ref, key_ref, value_ref, output_ref) = refs[:6]
    update_ref, layer_ref, queries, keys, values, contexts = refs[6:]
    own = lax.axis_index("seq")
    seq, _, col_dev, lanes = parts_ref.shape
    seq_dev, _, width = update_ref.shape
    rows = seq_dev * col_dev
    seqs = seq * seq_dev
    for place, field_ref in enumerate(fields):
        source = own ^ place
        context = []
        for half in range(seq_dev // HEADS):
            heads = [
                parts_ref[head, half * seq + source].astype(jnp.float32) for head in range(HEADS)
            ]
            context += swap_groups(heads, HEAD_DIM)
        context = jnp.concatenate(context, axis=0).astype(jnp.bfloat16)
        update = project(context, row_output_ref[...]).astype(jnp.bfloat16)
        field = field_ref[...].reshape(rows, width)
        middle = (field.astype(jnp.float32) + update.astype(jnp.float32)).astype(jnp.bfloat16)
        normal = norm_rows(middle.astype(jnp.float32))
        here = slice(place * rows, (place + 1) * rows)
        keys[here, :] = project(normal, key_ref[...]).astype(jnp.bfloat16).astype(jnp.float32)
        values[here, :] = project(normal, value_ref[...]).astype(jnp.bfloat16).astype(jnp.float32)
        if place == 0:
            update_ref[...] = update.reshape(update_ref.shape)
            layer_ref[...] = middle.reshape(layer_ref.shape)
            queries[...] = (
                project(normal, query_ref[...]).astype(jnp.bfloat16).astype(jnp.float32)
            )
    group = lanes // seqs
    head_of = lax.broadcasted_iota(jnp.int32, (seq_dev, lanes), 1) // HEAD_DIM
    size = group * seqs
    row_column = lax.broadcasted_iota(jnp.int32, (group * HEADS * seq_dev, size), 0) // (
        HEADS * seq_dev
    )
    same = row_column == lax.broadcasted_iota(jnp.int32, row_column.shape, 1) // seqs
    for first in range(0, col_dev, group):
        query, key, value = [], [], []
        for column in range(first, first + group):
            row = queries[pl.ds(column, seq_dev, stride=col_dev), :]
            query += [jnp.where(head_of == head, row, 0.0) for head in range(HEADS)]
            key.append(keys[pl.ds(column, seqs, stride=col_dev), :])
            value.append(values[pl.ds(column, seqs, stride=col_dev), :])
        query, key, value = (
            jnp.concatenate(part, axis=0).astype(jnp.bfloat16) for part in (query, key, value)
        )
        scores = jnp.where(
            same, contract_last(query, key) * float(HEAD_DIM) ** (-0.5), -jnp.inf
        )
        weights = jnp.exp(scores - jnp.max(scores, axis=-1, keepdims=True))
        probs = (weights / jnp.sum(weights, axis=-1, keepdims=True)).astype(jnp.bfloat16)
        context = project(probs, value)
        for place in range(group):
            total = jnp.zeros((seq_dev, lanes), jnp.float32)
            for head in range(HEADS):
                at = (place * HEADS + head) * seq_dev
                total = jnp.where(head_of == head, context[at : at + seq_dev], total)
            contexts[pl.ds(first + place, seq_dev, stride=col_dev), :] = total
    layer = layer_ref[...].reshape(rows, width).astype(jnp.float32) + project(
        contexts[...].astype(jnp.bfloat16), output_ref[...]
    )
    layer_ref[...] = layer.astype(jnp.bfloat16).reshape(layer_ref.shape)


def by_head(
    alignment,
    row_query,
    row_key,
    row_value,
    row_output,
    column_query,
    column_key,
    column_value,
    column_output,
):
    seq_dev, col_dev, _ = alignment.shape
    inner = row_query.shape[1]
    seq, col = lax.axis_size("seq"), lax.axis_size("col")
    scale = float(HEAD_DIM * seq_dev * seq) ** (-0.5)
    bf16, f32 = jnp.bfloat16, jnp.float32
    vmem = pl.BlockSpec(memory_space=pltpu.VMEM)
    grant = pltpu.CompilerParams(vmem_limit_bytes=8 << 20)
    fields = {0: alignment}
    for place in range(seq - 1, 0, -1):
        fields[place] = lax.ppermute(alignment, "seq", [(i, i ^ place) for i in range(seq)])
    fields = [fields[place] for place in range(seq)]
    sources = (alignment, row_key, row_value)
    blocks = pl.pallas_call(
        project_kernel,
        out_shape=jax.ShapeDtypeStruct((seq, col // 2, 2, 2, col_dev, inner), bf16),
        in_specs=[pl.BlockSpec(memory_space=pltpu.HBM)] * 3,
        out_specs=vmem,
        scratch_shapes=[pltpu.VMEM(source.shape, bf16) for source in sources]
        + [pltpu.SemaphoreType.DMA((3,))],
        compiler_params=grant,
        name="project",
    )(*(pltpu.with_memory_space_constraint(source, pltpu.HBM) for source in sources))
    mine = lax.all_to_all(blocks.reshape(seq * col, 2, col_dev, inner), ("seq", "col"), 0, 0)
    other = lax.ppermute(mine, "col", [(i, i ^ 1) for i in range(col)])
    shape = (seq, col, 2, col_dev, inner)
    mine, other = mine.reshape(shape), other.reshape(shape)
    halves = seq_dev // HEADS
    queries, logits = pl.pallas_call(
        query_kernel,
        out_shape=(
            jax.ShapeDtypeStruct((halves, seq, col_dev, inner), bf16),
            jax.ShapeDtypeStruct((col_dev, col * col_dev), f32),
        ),
        in_specs=[vmem] * (seq + 2),
        out_specs=(vmem, vmem),
        compiler_params=grant,
        name="query",
    )(*fields, row_query, mine)
    parts = pl.pallas_call(
        functools.partial(attend_kernel, scale),
        out_shape=jax.ShapeDtypeStruct((seq, halves * seq, col_dev, inner), bf16),
        in_specs=[vmem] * 4,
        out_specs=vmem,
        compiler_params=grant,
        name="attend",
    )(mine, other, queries, logits)
    parts = lax.all_to_all(parts, "seq", 0, 0)
    total = seq * seq_dev * col_dev
    local = seq_dev * col_dev
    like = jax.ShapeDtypeStruct(alignment.shape, bf16)
    return pl.pallas_call(
        finish_kernel,
        out_shape=(like, like),
        in_specs=[vmem] * (seq + 6),
        out_specs=(vmem, vmem),
        scratch_shapes=[
            pltpu.VMEM((local, inner), f32),
            pltpu.VMEM((total, inner), f32),
            pltpu.VMEM((total, inner), f32),
            pltpu.VMEM((local, inner), f32),
        ],
        compiler_params=grant,
        name="finish",
    )(*fields, parts, row_output, column_query, column_key, column_value, column_output)


def suits_by_head(seq, col, seq_dev, col_dev, width, inner):
    return (
        seq == HEADS
        and col % 2 == 0
        and seq_dev == 2 * HEADS
        and col_dev % 16 == 0
        and inner == HEADS * HEAD_DIM
        and inner == 128
        and width % inner == 0
        and inner % (seq * seq_dev) == 0
        and col_dev % (inner // (seq * seq_dev)) == 0
        and seq * seq_dev * col_dev <= 1024
        and col * col_dev <= 512
    )


def solution(mesh):
    def choose(*args):
        seq_dev, col_dev, width = args[0].shape
        sizes = (mesh.shape["seq"], mesh.shape["col"], seq_dev, col_dev, width, args[1].shape[1])
        return (by_head if suits_by_head(*sizes) else on_device)(*args)

    return jax.shard_map(
        choose,
        mesh=mesh,
        in_specs=(P("seq", "col", None), P(), P(), P(), P(), P(), P(), P(), P()),
        out_specs=(P("seq", "col", None), P("seq", "col", None)),
        check_vma=False,
    )
```

```python
import functools

import jax
import jax.numpy as jnp
from jax import lax
from jax.experimental import pallas as pl
from jax.experimental.pallas import tpu as pltpu
from jax.sharding import PartitionSpec as P


HEADS = 4
HEAD_DIM = 32


def layer_norm(field):
    values = field.astype(jnp.float32)
    mean = jnp.mean(values, axis=-1, keepdims=True)
    centred = values - mean
    variance = jnp.mean(centred * centred, axis=-1, keepdims=True)
    return (centred * lax.rsqrt(variance + 1e-05)).astype(jnp.bfloat16)


def project(field, weight):
    return jnp.dot(field, weight, preferred_element_type=jnp.float32)


def gather(block, axis, groups=None, size=None):
    size = lax.axis_size(axis) if size is None else size
    copies = jnp.broadcast_to(block[None], (size,) + block.shape)
    return lax.all_to_all(copies, axis, 0, 0, axis_index_groups=groups)


def gather_columns(block):
    size = lax.axis_size("col")
    if size % 2 or size == 2:
        return gather(block, "col")
    groups = [[i for i in range(size) if i % 2 == parity] for parity in (0, 1)]
    mine = gather(block, "col", groups, size // 2)
    other = lax.ppermute(mine, "col", [(i, i ^ 1) for i in range(size)])
    return jnp.concatenate([mine, other], axis=0)


def column_attend(queries, keys, values):
    seq_rows, columns, inner = queries.shape
    query_heads = queries.reshape(seq_rows, columns, HEADS, HEAD_DIM)
    key_heads = keys.reshape(keys.shape[0], columns, HEADS, HEAD_DIM)
    value_heads = values.reshape(values.shape[0], columns, HEADS, HEAD_DIM)
    scores = jnp.einsum(
        "schd,tchd->chst", query_heads, key_heads, preferred_element_type=jnp.float32
    ) * float(HEAD_DIM) ** (-0.5)
    weights = jax.nn.softmax(scores, axis=-1).astype(jnp.bfloat16)
    context = jnp.einsum(
        "chst,tchd->schd", weights, value_heads, preferred_element_type=jnp.float32
    )
    return context.reshape(seq_rows, columns, inner).astype(jnp.bfloat16)


def on_device(
    alignment,
    row_query,
    row_key,
    row_value,
    row_output,
    column_query,
    column_key,
    column_value,
    column_output,
):
    seq_dev, col_dev, _ = alignment.shape
    inner = row_query.shape[1]
    scale = float(HEAD_DIM * seq_dev * lax.axis_size("seq")) ** (-0.5)
    normed = layer_norm(alignment)
    queries = project(normed, row_query).astype(jnp.bfloat16)
    key_value = project(normed, jnp.concatenate([row_key, row_value], axis=1)).astype(jnp.bfloat16)
    query_heads = queries.reshape(seq_dev, col_dev, HEADS, HEAD_DIM)
    every = gather_columns(key_value)
    key_heads = every[..., :inner].reshape(every.shape[0], seq_dev, col_dev, HEADS, HEAD_DIM)
    value_heads = every[..., inner:].reshape(every.shape[0], seq_dev, col_dev, HEADS, HEAD_DIM)
    partial_value = jnp.einsum(
        "sihd,gsjhd->higj", query_heads, key_heads, preferred_element_type=jnp.float32
    )
    shape = partial_value.shape
    partial_value = partial_value.reshape(shape[0], shape[1], -1)
    logits = jnp.sum(gather(partial_value, "seq"), axis=0) * scale
    probs = jax.nn.softmax(logits, axis=-1).astype(jnp.bfloat16).reshape(shape)
    context = jnp.einsum("higj,gsjhd->sihd", probs, value_heads, preferred_element_type=jnp.float32)
    context = context.reshape(seq_dev, col_dev, inner).astype(jnp.bfloat16)
    row_update = project(context, row_output).astype(jnp.bfloat16)
    middle = (alignment.astype(jnp.float32) + row_update.astype(jnp.float32)).astype(jnp.bfloat16)
    column_normed = layer_norm(middle)
    column_queries = project(column_normed, column_query).astype(jnp.bfloat16)
    column_pair = project(column_normed, jnp.concatenate([column_key, column_value], axis=1))
    every = gather(column_pair.astype(jnp.bfloat16), "seq")
    every = every.reshape((-1,) + every.shape[2:])
    column_context = column_attend(column_queries, every[..., :inner], every[..., inner:])
    layer_output = (middle.astype(jnp.float32) + project(column_context, column_output)).astype(
        jnp.bfloat16
    )
    return (row_update, layer_output)


def norm_rows(values):
    mean = jnp.mean(values, axis=-1, keepdims=True)
    centred = values - mean
    variance = jnp.mean(centred * centred, axis=-1, keepdims=True)
    return (centred * lax.rsqrt(variance + 1e-05)).astype(jnp.bfloat16)


def swap_groups(arrays, group):
    lanes = arrays[0].shape[-1]
    index = lax.broadcasted_iota(jnp.int32, arrays[0].shape, 1) // group
    arrays = list(arrays)
    step = len(arrays) // 2
    while step:
        low = (index // step) % 2 == 0
        for first in range(len(arrays)):
            if (first // step) % 2 == 0:
                one, two = arrays[first], arrays[first + step]
                shift = step * group
                arrays[first] = jnp.where(low, one, pltpu.roll(two, shift, 1))
                arrays[first + step] = jnp.where(low, pltpu.roll(one, lanes - shift, 1), two)
        step //= 2
    return arrays


def contract_last(left, right):
    return lax.dot_general(
        left, right, (((1,), (1,)), ((), ())), preferred_element_type=jnp.float32
    )


def project_kernel(*refs):
    sources, out_ref, held, sems = refs[:3], refs[3], refs[4:7], refs[7]
    copies = [
        pltpu.make_async_copy(source, ref, sems.at[place])
        for place, (source, ref) in enumerate(zip(sources, held))
    ]
    for copy in copies:
        copy.start()
    field_ref, key_ref, value_ref = held
    seq_dev, col_dev, width = field_ref.shape
    heads, chips, cores = out_ref.shape[:3]
    copies[0].wait()
    normed = norm_rows(field_ref[...].astype(jnp.float32).reshape(seq_dev * col_dev, width))
    for kind, weight_ref in enumerate((key_ref, value_ref)):
        copies[kind + 1].wait()
        rows = project(normed, weight_ref[...])
        for core in range(cores):
            first = core * heads
            tiles = [
                rows[(first + place) * col_dev : (first + place + 1) * col_dev]
                for place in range(heads)
            ]
            for head, tile in enumerate(swap_groups(tiles, HEAD_DIM)):
                tile = tile.astype(jnp.bfloat16)
                for chip in range(chips):
                    out_ref[head, chip, core, kind] = tile


def query_kernel(*refs):
    fields, (weight_ref, mine_ref, query_ref, logits_ref) = refs[:-4], refs[-4:]
    own, half = lax.axis_index("seq"), lax.rem(lax.axis_index("col"), 2)
    seq_dev, col_dev, width = fields[0].shape
    seq, col, _, _, lanes = mine_ref.shape
    group = lax.broadcasted_iota(jnp.int32, weight_ref.shape, 1) // HEAD_DIM
    weight = weight_ref[...].astype(jnp.float32)
    spread = []
    for place in range(HEADS):
        shift = lax.rem((place + HEADS - own) * HEAD_DIM, lanes)
        spread.append(jnp.where(group == place, pltpu.roll(weight, shift, 1), 0.0))
    spread = jnp.concatenate(spread, axis=0).astype(jnp.bfloat16)
    normed = []
    for field_ref in fields:
        rows = norm_rows(field_ref[...].astype(jnp.float32).reshape(seq_dev * col_dev, width))
        for first in range(0, seq_dev, HEADS):
            normed.append(
                jnp.concatenate(
                    [
                        rows[place * col_dev : (place + 1) * col_dev]
                        for place in range(first, first + HEADS)
                    ],
                    axis=1,
                )
            )
    queries = project(jnp.concatenate(normed, axis=0), spread).astype(jnp.bfloat16)
    halves = seq_dev // HEADS
    for place in range(seq):
        for part in range(halves):
            start = (place * halves + part) * col_dev
            query_ref[part, own ^ place] = queries[start : start + col_dev]
    logits = jnp.zeros(logits_ref.shape, jnp.float32)
    for source in range(seq):
        keys = mine_ref[source, :, 0].reshape(col * col_dev, lanes)
        logits += contract_last(query_ref[half, source], keys)
    logits_ref[...] = logits


def attend_kernel(scale, mine_ref, other_ref, query_ref, logits_ref, out_ref):
    half = lax.rem(lax.axis_index("col"), 2)
    seq, col, _, col_dev, lanes = mine_ref.shape
    logits = logits_ref[...]
    for source in range(seq):
        keys = other_ref[source, :, 0].reshape(col * col_dev, lanes)
        logits += contract_last(query_ref[1 - half, source], keys)
    logits = logits * scale
    weights = jnp.exp(logits - jnp.max(logits, axis=-1, keepdims=True))
    probs = (weights / jnp.sum(weights, axis=-1, keepdims=True)).astype(jnp.bfloat16)
    for ref, part in ((mine_ref, half), (other_ref, 1 - half)):
        for source in range(seq):
            values = ref[source, :, 1].reshape(col * col_dev, lanes)
            context = project(probs, values).astype(jnp.bfloat16)
            for copy in range(seq):
                out_ref[copy, part * seq + source] = context


def finish_kernel(*refs):
    fields, refs = refs[:-13], refs[-13:]
    (parts_ref, row_output_ref, query_ref, key_ref, value_ref, output_ref) = refs[:6]
    update_ref, layer_ref, middles, queries, keys, values, contexts = refs[6:]
    own = lax.axis_index("seq")
    seq, _, col_dev, lanes = parts_ref.shape
    seq_dev, _, width = update_ref.shape
    rows = seq_dev * col_dev
    seqs = seq * seq_dev
    pair = jnp.concatenate([key_ref[...], value_ref[...]], axis=1)
    for place, field_ref in enumerate(fields):
        source = own ^ place
        context = []
        for half in range(seq_dev // HEADS):
            heads = [
                parts_ref[head, half * seq + source].astype(jnp.float32) for head in range(HEADS)
            ]
            context += swap_groups(heads, HEAD_DIM)
        context = jnp.concatenate(context, axis=0).astype(jnp.bfloat16)
        update = project(context, row_output_ref[...])
        middle = field_ref[...].reshape(rows, width).astype(jnp.float32) + update
        normal = norm_rows(middle)
        here = slice(place * rows, (place + 1) * rows)
        both = project(normal, pair)
        keys[here, :] = both[:, :lanes]
        values[here, :] = both[:, lanes:]
        if place == 0:
            update_ref[...] = update.astype(jnp.bfloat16).reshape(update_ref.shape)
            middles[...] = middle
            queries[...] = project(normal, query_ref[...]) * float(HEAD_DIM) ** (-0.5)
    group = lanes // seqs
    head_of = lax.broadcasted_iota(jnp.int32, (seq_dev, lanes), 1) // HEAD_DIM
    size = group * seqs
    row_column = lax.broadcasted_iota(jnp.int32, (group * HEADS * seq_dev, size), 0) // (
        HEADS * seq_dev
    )
    same = row_column == lax.broadcasted_iota(jnp.int32, row_column.shape, 1) // seqs
    ones = jnp.ones((size, lanes), jnp.bfloat16)
    for first in range(0, col_dev, group):
        query, key, value = [], [], []
        for column in range(first, first + group):
            row = queries[pl.ds(column, seq_dev, stride=col_dev), :]
            query += [jnp.where(head_of == head, row, 0.0) for head in range(HEADS)]
            key.append(keys[pl.ds(column, seqs, stride=col_dev), :])
            value.append(values[pl.ds(column, seqs, stride=col_dev), :])
        query, key, value = (
            jnp.concatenate(part, axis=0).astype(jnp.bfloat16) for part in (query, key, value)
        )
        scores = jnp.where(same, contract_last(query, key), -jnp.inf)
        weights = jnp.exp(scores - jnp.max(scores, axis=-1, keepdims=True))
        both = project(weights.astype(jnp.bfloat16), jnp.concatenate([value, ones], axis=1))
        for place in range(group):
            above = jnp.zeros((seq_dev, lanes), jnp.float32)
            below = jnp.ones((seq_dev, lanes), jnp.float32)
            for head in range(HEADS):
                at = (place * HEADS + head) * seq_dev
                above = jnp.where(head_of == head, both[at : at + seq_dev, :lanes], above)
                below = jnp.where(head_of == head, both[at : at + seq_dev, lanes:], below)
            contexts[pl.ds(first + place, seq_dev, stride=col_dev), :] = above / below
    layer = middles[...] + project(contexts[...].astype(jnp.bfloat16), output_ref[...])
    layer_ref[...] = layer.astype(jnp.bfloat16).reshape(layer_ref.shape)


def by_head(
    alignment,
    row_query,
    row_key,
    row_value,
    row_output,
    column_query,
    column_key,
    column_value,
    column_output,
):
    seq_dev, col_dev, width = alignment.shape
    inner = row_query.shape[1]
    seq, col = lax.axis_size("seq"), lax.axis_size("col")
    scale = float(HEAD_DIM * seq_dev * seq) ** (-0.5)
    bf16, f32 = jnp.bfloat16, jnp.float32
    vmem = pl.BlockSpec(memory_space=pltpu.VMEM)
    grant = pltpu.CompilerParams(vmem_limit_bytes=8 << 20)
    fields = {0: alignment}
    for place in range(seq - 1, 0, -1):
        fields[place] = lax.ppermute(alignment, "seq", [(i, i ^ place) for i in range(seq)])
    fields = [fields[place] for place in range(seq)]
    sources = (alignment, row_key, row_value)
    blocks = pl.pallas_call(
        project_kernel,
        out_shape=jax.ShapeDtypeStruct((seq, col // 2, 2, 2, col_dev, inner), bf16),
        in_specs=[pl.BlockSpec(memory_space=pltpu.HBM)] * 3,
        out_specs=vmem,
        scratch_shapes=[pltpu.VMEM(source.shape, bf16) for source in sources]
        + [pltpu.SemaphoreType.DMA((3,))],
        compiler_params=grant,
        name="project",
    )(*(pltpu.with_memory_space_constraint(source, pltpu.HBM) for source in sources))
    mine = lax.all_to_all(blocks.reshape(seq * col, 2, col_dev, inner), ("seq", "col"), 0, 0)
    other = lax.ppermute(mine, "col", [(i, i ^ 1) for i in range(col)])
    shape = (seq, col, 2, col_dev, inner)
    mine, other = mine.reshape(shape), other.reshape(shape)
    halves = seq_dev // HEADS
    queries, logits = pl.pallas_call(
        query_kernel,
        out_shape=(
            jax.ShapeDtypeStruct((halves, seq, col_dev, inner), bf16),
            jax.ShapeDtypeStruct((col_dev, col * col_dev), f32),
        ),
        in_specs=[vmem] * (seq + 2),
        out_specs=(vmem, vmem),
        compiler_params=grant,
        name="query",
    )(*fields, row_query, mine)
    parts = pl.pallas_call(
        functools.partial(attend_kernel, scale),
        out_shape=jax.ShapeDtypeStruct((seq, halves * seq, col_dev, inner), bf16),
        in_specs=[vmem] * 4,
        out_specs=vmem,
        compiler_params=grant,
        name="attend",
    )(mine, other, queries, logits)
    parts = lax.all_to_all(parts, "seq", 0, 0)
    total = seq * seq_dev * col_dev
    local = seq_dev * col_dev
    like = jax.ShapeDtypeStruct(alignment.shape, bf16)
    return pl.pallas_call(
        finish_kernel,
        out_shape=(like, like),
        in_specs=[vmem] * (seq + 6),
        out_specs=(vmem, vmem),
        scratch_shapes=[
            pltpu.VMEM((local, width), f32),
            pltpu.VMEM((local, inner), f32),
            pltpu.VMEM((total, inner), f32),
            pltpu.VMEM((total, inner), f32),
            pltpu.VMEM((local, inner), f32),
        ],
        compiler_params=grant,
        name="finish",
    )(*fields, parts, row_output, column_query, column_key, column_value, column_output)


def suits_by_head(seq, col, seq_dev, col_dev, width, inner):
    return (
        seq == HEADS
        and col % 2 == 0
        and seq_dev == 2 * HEADS
        and col_dev % 16 == 0
        and inner == HEADS * HEAD_DIM
        and inner == 128
        and width % inner == 0
        and inner % (seq * seq_dev) == 0
        and col_dev % (inner // (seq * seq_dev)) == 0
        and seq * seq_dev * col_dev <= 1024
        and col * col_dev <= 512
    )


def solution(mesh):
    def choose(*args):
        seq_dev, col_dev, width = args[0].shape
        sizes = (mesh.shape["seq"], mesh.shape["col"], seq_dev, col_dev, width, args[1].shape[1])
        return (by_head if suits_by_head(*sizes) else on_device)(*args)

    return jax.shard_map(
        choose,
        mesh=mesh,
        in_specs=(P("seq", "col", None), P(), P(), P(), P(), P(), P(), P(), P()),
        out_specs=(P("seq", "col", None), P("seq", "col", None)),
        check_vma=False,
    )
```

```python
import functools

import jax
import jax.numpy as jnp
from jax import lax
from jax.experimental import pallas as pl
from jax.experimental.pallas import tpu as pltpu
from jax.sharding import PartitionSpec as P


HEADS = 4
HEAD_DIM = 32


def layer_norm(field):
    values = field.astype(jnp.float32)
    mean = jnp.mean(values, axis=-1, keepdims=True)
    centred = values - mean
    variance = jnp.mean(centred * centred, axis=-1, keepdims=True)
    return (centred * lax.rsqrt(variance + 1e-05)).astype(jnp.bfloat16)


def project(field, weight):
    return jnp.dot(field, weight, preferred_element_type=jnp.float32)


def gather(block, axis, groups=None, size=None):
    size = lax.axis_size(axis) if size is None else size
    copies = jnp.broadcast_to(block[None], (size,) + block.shape)
    return lax.all_to_all(copies, axis, 0, 0, axis_index_groups=groups)


def gather_columns(block):
    size = lax.axis_size("col")
    if size % 2 or size == 2:
        return gather(block, "col")
    groups = [[i for i in range(size) if i % 2 == parity] for parity in (0, 1)]
    mine = gather(block, "col", groups, size // 2)
    other = lax.ppermute(mine, "col", [(i, i ^ 1) for i in range(size)])
    return jnp.concatenate([mine, other], axis=0)


def column_attend(queries, keys, values):
    seq_rows, columns, inner = queries.shape
    query_heads = queries.reshape(seq_rows, columns, HEADS, HEAD_DIM)
    key_heads = keys.reshape(keys.shape[0], columns, HEADS, HEAD_DIM)
    value_heads = values.reshape(values.shape[0], columns, HEADS, HEAD_DIM)
    scores = jnp.einsum(
        "schd,tchd->chst", query_heads, key_heads, preferred_element_type=jnp.float32
    ) * float(HEAD_DIM) ** (-0.5)
    weights = jax.nn.softmax(scores, axis=-1).astype(jnp.bfloat16)
    context = jnp.einsum(
        "chst,tchd->schd", weights, value_heads, preferred_element_type=jnp.float32
    )
    return context.reshape(seq_rows, columns, inner).astype(jnp.bfloat16)


def on_device(
    alignment,
    row_query,
    row_key,
    row_value,
    row_output,
    column_query,
    column_key,
    column_value,
    column_output,
):
    seq_dev, col_dev, _ = alignment.shape
    inner = row_query.shape[1]
    scale = float(HEAD_DIM * seq_dev * lax.axis_size("seq")) ** (-0.5)
    normed = layer_norm(alignment)
    queries = project(normed, row_query).astype(jnp.bfloat16)
    key_value = project(normed, jnp.concatenate([row_key, row_value], axis=1)).astype(jnp.bfloat16)
    query_heads = queries.reshape(seq_dev, col_dev, HEADS, HEAD_DIM)
    every = gather_columns(key_value)
    key_heads = every[..., :inner].reshape(every.shape[0], seq_dev, col_dev, HEADS, HEAD_DIM)
    value_heads = every[..., inner:].reshape(every.shape[0], seq_dev, col_dev, HEADS, HEAD_DIM)
    partial_value = jnp.einsum(
        "sihd,gsjhd->higj", query_heads, key_heads, preferred_element_type=jnp.float32
    )
    shape = partial_value.shape
    partial_value = partial_value.reshape(shape[0], shape[1], -1)
    logits = jnp.sum(gather(partial_value, "seq"), axis=0) * scale
    probs = jax.nn.softmax(logits, axis=-1).astype(jnp.bfloat16).reshape(shape)
    context = jnp.einsum("higj,gsjhd->sihd", probs, value_heads, preferred_element_type=jnp.float32)
    context = context.reshape(seq_dev, col_dev, inner).astype(jnp.bfloat16)
    row_update = project(context, row_output).astype(jnp.bfloat16)
    middle = (alignment.astype(jnp.float32) + row_update.astype(jnp.float32)).astype(jnp.bfloat16)
    column_normed = layer_norm(middle)
    column_queries = project(column_normed, column_query).astype(jnp.bfloat16)
    column_pair = project(column_normed, jnp.concatenate([column_key, column_value], axis=1))
    every = gather(column_pair.astype(jnp.bfloat16), "seq")
    every = every.reshape((-1,) + every.shape[2:])
    column_context = column_attend(column_queries, every[..., :inner], every[..., inner:])
    layer_output = (middle.astype(jnp.float32) + project(column_context, column_output)).astype(
        jnp.bfloat16
    )
    return (row_update, layer_output)


def norm_rows(values):
    mean = jnp.mean(values, axis=-1, keepdims=True)
    centred = values - mean
    variance = jnp.mean(centred * centred, axis=-1, keepdims=True)
    return (centred * lax.rsqrt(variance + 1e-05)).astype(jnp.bfloat16)


def swap_groups(arrays, group):
    lanes = arrays[0].shape[-1]
    index = lax.broadcasted_iota(jnp.int32, arrays[0].shape, 1) // group
    arrays = list(arrays)
    step = len(arrays) // 2
    while step:
        low = (index // step) % 2 == 0
        for first in range(len(arrays)):
            if (first // step) % 2 == 0:
                one, two = arrays[first], arrays[first + step]
                shift = step * group
                arrays[first] = jnp.where(low, one, pltpu.roll(two, shift, 1))
                arrays[first + step] = jnp.where(low, pltpu.roll(one, lanes - shift, 1), two)
        step //= 2
    return arrays


def contract_last(left, right):
    return lax.dot_general(
        left, right, (((1,), (1,)), ((), ())), preferred_element_type=jnp.float32
    )


def gate_kernel(out_ref):
    out_ref[...] = jnp.zeros_like(out_ref)


def project_kernel(field_ref, key_ref, value_ref, gate_ref, out_ref):
    seq_dev, col_dev, width = field_ref.shape
    heads, chips, cores = out_ref.shape[:3]
    normed = norm_rows(field_ref[...].astype(jnp.float32).reshape(seq_dev * col_dev, width))
    for kind, weight_ref in enumerate((key_ref, value_ref)):
        rows = project(normed, weight_ref[...])
        for core in range(cores):
            first = core * heads
            tiles = [
                rows[(first + place) * col_dev : (first + place + 1) * col_dev]
                for place in range(heads)
            ]
            for head, tile in enumerate(swap_groups(tiles, HEAD_DIM)):
                tile = tile.astype(jnp.bfloat16)
                for chip in range(chips):
                    out_ref[head, chip, core, kind] = tile


def query_kernel(*refs):
    fields, (weight_ref, mine_ref, query_ref, logits_ref) = refs[:-4], refs[-4:]
    own, half = lax.axis_index("seq"), lax.rem(lax.axis_index("col"), 2)
    seq_dev, col_dev, width = fields[0].shape
    seq, col, _, _, lanes = mine_ref.shape
    group = lax.broadcasted_iota(jnp.int32, weight_ref.shape, 1) // HEAD_DIM
    weight = weight_ref[...].astype(jnp.float32)
    spread = []
    for place in range(HEADS):
        shift = lax.rem((place + HEADS - own) * HEAD_DIM, lanes)
        spread.append(jnp.where(group == place, pltpu.roll(weight, shift, 1), 0.0))
    spread = jnp.concatenate(spread, axis=0).astype(jnp.bfloat16)
    normed = []
    for field_ref in fields:
        rows = norm_rows(field_ref[...].astype(jnp.float32).reshape(seq_dev * col_dev, width))
        for first in range(0, seq_dev, HEADS):
            normed.append(
                jnp.concatenate(
                    [
                        rows[place * col_dev : (place + 1) * col_dev]
                        for place in range(first, first + HEADS)
                    ],
                    axis=1,
                )
            )
    queries = project(jnp.concatenate(normed, axis=0), spread).astype(jnp.bfloat16)
    halves = seq_dev // HEADS
    for place in range(seq):
        for part in range(halves):
            start = (place * halves + part) * col_dev
            query_ref[part, own ^ place] = queries[start : start + col_dev]
    logits = jnp.zeros(logits_ref.shape, jnp.float32)
    for source in range(seq):
        keys = mine_ref[source, :, 0].reshape(col * col_dev, lanes)
        logits += contract_last(query_ref[half, source], keys)
    logits_ref[...] = logits


def attend_kernel(scale, mine_ref, other_ref, query_ref, logits_ref, out_ref):
    half = lax.rem(lax.axis_index("col"), 2)
    seq, col, _, col_dev, lanes = mine_ref.shape
    logits = logits_ref[...]
    for source in range(seq):
        keys = other_ref[source, :, 0].reshape(col * col_dev, lanes)
        logits += contract_last(query_ref[1 - half, source], keys)
    logits = logits * scale
    weights = jnp.exp(logits - jnp.max(logits, axis=-1, keepdims=True))
    probs = (weights / jnp.sum(weights, axis=-1, keepdims=True)).astype(jnp.bfloat16)
    for ref, part in ((mine_ref, half), (other_ref, 1 - half)):
        for source in range(seq):
            values = ref[source, :, 1].reshape(col * col_dev, lanes)
            context = project(probs, values).astype(jnp.bfloat16)
            for copy in range(seq):
                out_ref[copy, part * seq + source] = context


def finish_kernel(*refs):
    fields, refs = refs[:-13], refs[-13:]
    (parts_ref, row_output_ref, query_ref, key_ref, value_ref, output_ref) = refs[:6]
    update_ref, layer_ref, middles, queries, keys, values, contexts = refs[6:]
    own = lax.axis_index("seq")
    seq, _, col_dev, lanes = parts_ref.shape
    seq_dev, _, width = update_ref.shape
    rows = seq_dev * col_dev
    seqs = seq * seq_dev
    pair = jnp.concatenate([key_ref[...], value_ref[...]], axis=1)
    for place, field_ref in enumerate(fields):
        source = own ^ place
        context = []
        for half in range(seq_dev // HEADS):
            heads = [
                parts_ref[head, half * seq + source].astype(jnp.float32) for head in range(HEADS)
            ]
            context += swap_groups(heads, HEAD_DIM)
        context = jnp.concatenate(context, axis=0).astype(jnp.bfloat16)
        update = project(context, row_output_ref[...])
        middle = field_ref[...].reshape(rows, width).astype(jnp.float32) + update
        normal = norm_rows(middle)
        here = slice(place * rows, (place + 1) * rows)
        both = project(normal, pair)
        keys[here, :] = both[:, :lanes]
        values[here, :] = both[:, lanes:]
        if place == 0:
            update_ref[...] = update.astype(jnp.bfloat16).reshape(update_ref.shape)
            middles[...] = middle
            queries[...] = project(normal, query_ref[...]) * float(HEAD_DIM) ** (-0.5)
    group = lanes // seqs
    head_of = lax.broadcasted_iota(jnp.int32, (seq_dev, lanes), 1) // HEAD_DIM
    size = group * seqs
    row_column = lax.broadcasted_iota(jnp.int32, (group * HEADS * seq_dev, size), 0) // (
        HEADS * seq_dev
    )
    same = row_column == lax.broadcasted_iota(jnp.int32, row_column.shape, 1) // seqs
    ones = jnp.ones((size, lanes), jnp.bfloat16)
    for first in range(0, col_dev, group):
        query, key, value = [], [], []
        for column in range(first, first + group):
            row = queries[pl.ds(column, seq_dev, stride=col_dev), :]
            query += [jnp.where(head_of == head, row, 0.0) for head in range(HEADS)]
            key.append(keys[pl.ds(column, seqs, stride=col_dev), :])
            value.append(values[pl.ds(column, seqs, stride=col_dev), :])
        query, key, value = (
            jnp.concatenate(part, axis=0).astype(jnp.bfloat16) for part in (query, key, value)
        )
        scores = jnp.where(same, contract_last(query, key), -jnp.inf)
        weights = jnp.exp(scores - jnp.max(scores, axis=-1, keepdims=True))
        both = project(weights.astype(jnp.bfloat16), jnp.concatenate([value, ones], axis=1))
        for place in range(group):
            above = jnp.zeros((seq_dev, lanes), jnp.float32)
            below = jnp.ones((seq_dev, lanes), jnp.float32)
            for head in range(HEADS):
                at = (place * HEADS + head) * seq_dev
                above = jnp.where(head_of == head, both[at : at + seq_dev, :lanes], above)
                below = jnp.where(head_of == head, both[at : at + seq_dev, lanes:], below)
            contexts[pl.ds(first + place, seq_dev, stride=col_dev), :] = above / below
    layer = middles[...] + project(contexts[...].astype(jnp.bfloat16), output_ref[...])
    layer_ref[...] = layer.astype(jnp.bfloat16).reshape(layer_ref.shape)


def by_head(
    alignment,
    row_query,
    row_key,
    row_value,
    row_output,
    column_query,
    column_key,
    column_value,
    column_output,
):
    seq_dev, col_dev, width = alignment.shape
    inner = row_query.shape[1]
    seq, col = lax.axis_size("seq"), lax.axis_size("col")
    scale = float(HEAD_DIM * seq_dev * seq) ** (-0.5)
    bf16, f32 = jnp.bfloat16, jnp.float32
    vmem = pl.BlockSpec(memory_space=pltpu.VMEM)
    grant = pltpu.CompilerParams(vmem_limit_bytes=8 << 20)
    gate = pl.pallas_call(
        gate_kernel,
        out_shape=jax.ShapeDtypeStruct((8, inner), f32),
        out_specs=vmem,
        compiler_params=grant,
        cost_estimate=pl.CostEstimate(flops=1 << 33, transcendentals=0, bytes_accessed=1 << 24),
        name="gate",
    )()
    fields = {0: alignment}
    for place in range(seq - 1, 0, -1):
        fields[place] = lax.ppermute(alignment, "seq", [(i, i ^ place) for i in range(seq)])
    fields = [fields[place] for place in range(seq)]
    blocks = pl.pallas_call(
        project_kernel,
        out_shape=jax.ShapeDtypeStruct((seq, col // 2, 2, 2, col_dev, inner), bf16),
        in_specs=[vmem] * 4,
        out_specs=vmem,
        compiler_params=grant,
        name="project",
    )(alignment, row_key, row_value, gate)
    mine = lax.all_to_all(blocks.reshape(seq * col, 2, col_dev, inner), ("seq", "col"), 0, 0)
    other = lax.ppermute(mine, "col", [(i, i ^ 1) for i in range(col)])
    shape = (seq, col, 2, col_dev, inner)
    mine, other = mine.reshape(shape), other.reshape(shape)
    halves = seq_dev // HEADS
    queries, logits = pl.pallas_call(
        query_kernel,
        out_shape=(
            jax.ShapeDtypeStruct((halves, seq, col_dev, inner), bf16),
            jax.ShapeDtypeStruct((col_dev, col * col_dev), f32),
        ),
        in_specs=[vmem] * (seq + 2),
        out_specs=(vmem, vmem),
        compiler_params=grant,
        name="query",
    )(*fields, row_query, mine)
    parts = pl.pallas_call(
        functools.partial(attend_kernel, scale),
        out_shape=jax.ShapeDtypeStruct((seq, halves * seq, col_dev, inner), bf16),
        in_specs=[vmem] * 4,
        out_specs=vmem,
        compiler_params=grant,
        name="attend",
    )(mine, other, queries, logits)
    parts = lax.all_to_all(parts, "seq", 0, 0)
    total = seq * seq_dev * col_dev
    local = seq_dev * col_dev
    like = jax.ShapeDtypeStruct(alignment.shape, bf16)
    return pl.pallas_call(
        finish_kernel,
        out_shape=(like, like),
        in_specs=[vmem] * (seq + 6),
        out_specs=(vmem, vmem),
        scratch_shapes=[
            pltpu.VMEM((local, width), f32),
            pltpu.VMEM((local, inner), f32),
            pltpu.VMEM((total, inner), f32),
            pltpu.VMEM((total, inner), f32),
            pltpu.VMEM((local, inner), f32),
        ],
        compiler_params=grant,
        name="finish",
    )(*fields, parts, row_output, column_query, column_key, column_value, column_output)


def suits_by_head(seq, col, seq_dev, col_dev, width, inner):
    return (
        seq == HEADS
        and col % 2 == 0
        and seq_dev == 2 * HEADS
        and col_dev % 16 == 0
        and inner == HEADS * HEAD_DIM
        and inner == 128
        and width % inner == 0
        and inner % (seq * seq_dev) == 0
        and col_dev % (inner // (seq * seq_dev)) == 0
        and seq * seq_dev * col_dev <= 1024
        and col * col_dev <= 512
    )


def solution(mesh):
    def choose(*args):
        seq_dev, col_dev, width = args[0].shape
        sizes = (mesh.shape["seq"], mesh.shape["col"], seq_dev, col_dev, width, args[1].shape[1])
        return (by_head if suits_by_head(*sizes) else on_device)(*args)

    return jax.shard_map(
        choose,
        mesh=mesh,
        in_specs=(P("seq", "col", None), P(), P(), P(), P(), P(), P(), P(), P()),
        out_specs=(P("seq", "col", None), P("seq", "col", None)),
        check_vma=False,
    )
```

```python
import functools

import jax
import jax.numpy as jnp
from jax import lax
from jax.experimental import pallas as pl
from jax.experimental.pallas import tpu as pltpu
from jax.sharding import PartitionSpec as P


HEADS = 4
HEAD_DIM = 32


def layer_norm(field):
    values = field.astype(jnp.float32)
    mean = jnp.mean(values, axis=-1, keepdims=True)
    centred = values - mean
    variance = jnp.mean(centred * centred, axis=-1, keepdims=True)
    return (centred * lax.rsqrt(variance + 1e-05)).astype(jnp.bfloat16)


def project(field, weight):
    return jnp.dot(field, weight, preferred_element_type=jnp.float32)


def gather(block, axis, groups=None, size=None):
    size = lax.axis_size(axis) if size is None else size
    copies = jnp.broadcast_to(block[None], (size,) + block.shape)
    return lax.all_to_all(copies, axis, 0, 0, axis_index_groups=groups)


def gather_columns(block):
    size = lax.axis_size("col")
    if size % 2 or size == 2:
        return gather(block, "col")
    groups = [[i for i in range(size) if i % 2 == parity] for parity in (0, 1)]
    mine = gather(block, "col", groups, size // 2)
    other = lax.ppermute(mine, "col", [(i, i ^ 1) for i in range(size)])
    return jnp.concatenate([mine, other], axis=0)


def column_attend(queries, keys, values):
    seq_rows, columns, inner = queries.shape
    query_heads = queries.reshape(seq_rows, columns, HEADS, HEAD_DIM)
    key_heads = keys.reshape(keys.shape[0], columns, HEADS, HEAD_DIM)
    value_heads = values.reshape(values.shape[0], columns, HEADS, HEAD_DIM)
    scores = jnp.einsum(
        "schd,tchd->chst", query_heads, key_heads, preferred_element_type=jnp.float32
    ) * float(HEAD_DIM) ** (-0.5)
    weights = jax.nn.softmax(scores, axis=-1).astype(jnp.bfloat16)
    context = jnp.einsum(
        "chst,tchd->schd", weights, value_heads, preferred_element_type=jnp.float32
    )
    return context.reshape(seq_rows, columns, inner).astype(jnp.bfloat16)


def on_device(
    alignment,
    row_query,
    row_key,
    row_value,
    row_output,
    column_query,
    column_key,
    column_value,
    column_output,
):
    seq_dev, col_dev, _ = alignment.shape
    inner = row_query.shape[1]
    scale = float(HEAD_DIM * seq_dev * lax.axis_size("seq")) ** (-0.5)
    normed = layer_norm(alignment)
    queries = project(normed, row_query).astype(jnp.bfloat16)
    key_value = project(normed, jnp.concatenate([row_key, row_value], axis=1)).astype(jnp.bfloat16)
    query_heads = queries.reshape(seq_dev, col_dev, HEADS, HEAD_DIM)
    every = gather_columns(key_value)
    key_heads = every[..., :inner].reshape(every.shape[0], seq_dev, col_dev, HEADS, HEAD_DIM)
    value_heads = every[..., inner:].reshape(every.shape[0], seq_dev, col_dev, HEADS, HEAD_DIM)
    partial_value = jnp.einsum(
        "sihd,gsjhd->higj", query_heads, key_heads, preferred_element_type=jnp.float32
    )
    shape = partial_value.shape
    partial_value = partial_value.reshape(shape[0], shape[1], -1)
    logits = jnp.sum(gather(partial_value, "seq"), axis=0) * scale
    probs = jax.nn.softmax(logits, axis=-1).astype(jnp.bfloat16).reshape(shape)
    context = jnp.einsum("higj,gsjhd->sihd", probs, value_heads, preferred_element_type=jnp.float32)
    context = context.reshape(seq_dev, col_dev, inner).astype(jnp.bfloat16)
    row_update = project(context, row_output).astype(jnp.bfloat16)
    middle = (alignment.astype(jnp.float32) + row_update.astype(jnp.float32)).astype(jnp.bfloat16)
    column_normed = layer_norm(middle)
    column_queries = project(column_normed, column_query).astype(jnp.bfloat16)
    column_pair = project(column_normed, jnp.concatenate([column_key, column_value], axis=1))
    every = gather(column_pair.astype(jnp.bfloat16), "seq")
    every = every.reshape((-1,) + every.shape[2:])
    column_context = column_attend(column_queries, every[..., :inner], every[..., inner:])
    layer_output = (middle.astype(jnp.float32) + project(column_context, column_output)).astype(
        jnp.bfloat16
    )
    return (row_update, layer_output)


def norm_rows(values):
    mean = jnp.mean(values, axis=-1, keepdims=True)
    centred = values - mean
    variance = jnp.mean(centred * centred, axis=-1, keepdims=True)
    return (centred * lax.rsqrt(variance + 1e-05)).astype(jnp.bfloat16)


def swap_groups(arrays, group):
    lanes = arrays[0].shape[-1]
    index = lax.broadcasted_iota(jnp.int32, arrays[0].shape, 1) // group
    arrays = list(arrays)
    step = len(arrays) // 2
    while step:
        low = (index // step) % 2 == 0
        for first in range(len(arrays)):
            if (first // step) % 2 == 0:
                one, two = arrays[first], arrays[first + step]
                shift = step * group
                arrays[first] = jnp.where(low, one, pltpu.roll(two, shift, 1))
                arrays[first + step] = jnp.where(low, pltpu.roll(one, lanes - shift, 1), two)
        step //= 2
    return arrays


def contract_last(left, right):
    return lax.dot_general(
        left, right, (((1,), (1,)), ((), ())), preferred_element_type=jnp.float32
    )


def gate_kernel(out_ref):
    out_ref[...] = jnp.zeros_like(out_ref)


def project_kernel(field_ref, key_ref, value_ref, gate_ref, out_ref):
    seq_dev, col_dev, width = field_ref.shape
    heads, chips, cores = out_ref.shape[:3]
    normed = norm_rows(field_ref[...].astype(jnp.float32).reshape(seq_dev * col_dev, width))
    for kind, weight_ref in enumerate((key_ref, value_ref)):
        rows = project(normed, weight_ref[...])
        for core in range(cores):
            first = core * heads
            tiles = [
                rows[(first + place) * col_dev : (first + place + 1) * col_dev]
                for place in range(heads)
            ]
            for head, tile in enumerate(swap_groups(tiles, HEAD_DIM)):
                tile = tile.astype(jnp.bfloat16)
                for chip in range(chips):
                    out_ref[head, chip, core, kind] = tile


def query_kernel(*refs):
    fields, (weight_ref, query_ref) = refs[:-2], refs[-2:]
    own = lax.axis_index("seq")
    seq_dev, col_dev, width = fields[0].shape
    seq, lanes = len(fields), weight_ref.shape[1]
    group = lax.broadcasted_iota(jnp.int32, weight_ref.shape, 1) // HEAD_DIM
    weight = weight_ref[...].astype(jnp.float32)
    spread = []
    for place in range(HEADS):
        shift = lax.rem((place + HEADS - own) * HEAD_DIM, lanes)
        spread.append(jnp.where(group == place, pltpu.roll(weight, shift, 1), 0.0))
    spread = jnp.concatenate(spread, axis=0).astype(jnp.bfloat16)
    normed = []
    for field_ref in fields:
        rows = norm_rows(field_ref[...].astype(jnp.float32).reshape(seq_dev * col_dev, width))
        for first in range(0, seq_dev, HEADS):
            normed.append(
                jnp.concatenate(
                    [
                        rows[place * col_dev : (place + 1) * col_dev]
                        for place in range(first, first + HEADS)
                    ],
                    axis=1,
                )
            )
    queries = project(jnp.concatenate(normed, axis=0), spread).astype(jnp.bfloat16)
    halves = seq_dev // HEADS
    for place in range(seq):
        for part in range(halves):
            start = (place * halves + part) * col_dev
            query_ref[part, own ^ place] = queries[start : start + col_dev]


def attend_kernel(scale, mine_ref, other_ref, query_ref, out_ref):
    half = lax.rem(lax.axis_index("col"), 2)
    seq, col, _, col_dev, lanes = mine_ref.shape
    logits = jnp.zeros((col_dev, col * col_dev), jnp.float32)
    for ref, part in ((mine_ref, half), (other_ref, 1 - half)):
        for source in range(seq):
            keys = ref[source, :, 0].reshape(col * col_dev, lanes)
            logits += contract_last(query_ref[part, source], keys)
    logits = logits * scale
    weights = jnp.exp(logits - jnp.max(logits, axis=-1, keepdims=True))
    probs = (weights / jnp.sum(weights, axis=-1, keepdims=True)).astype(jnp.bfloat16)
    for ref, part in ((mine_ref, half), (other_ref, 1 - half)):
        for source in range(seq):
            values = ref[source, :, 1].reshape(col * col_dev, lanes)
            context = project(probs, values).astype(jnp.bfloat16)
            for copy in range(seq):
                out_ref[copy, part * seq + source] = context


def finish_kernel(*refs):
    fields, refs = refs[:-13], refs[-13:]
    (parts_ref, row_output_ref, query_ref, key_ref, value_ref, output_ref) = refs[:6]
    update_ref, layer_ref, middles, queries, keys, values, contexts = refs[6:]
    own = lax.axis_index("seq")
    seq, _, col_dev, lanes = parts_ref.shape
    seq_dev, _, width = update_ref.shape
    rows = seq_dev * col_dev
    seqs = seq * seq_dev
    pair = jnp.concatenate([key_ref[...], value_ref[...]], axis=1)
    for place, field_ref in enumerate(fields):
        source = own ^ place
        context = []
        for half in range(seq_dev // HEADS):
            heads = [
                parts_ref[head, half * seq + source].astype(jnp.float32) for head in range(HEADS)
            ]
            context += swap_groups(heads, HEAD_DIM)
        context = jnp.concatenate(context, axis=0).astype(jnp.bfloat16)
        update = project(context, row_output_ref[...])
        middle = field_ref[...].reshape(rows, width).astype(jnp.float32) + update
        normal = norm_rows(middle)
        here = slice(place * rows, (place + 1) * rows)
        both = project(normal, pair)
        keys[here, :] = both[:, :lanes]
        values[here, :] = both[:, lanes:]
        if place == 0:
            update_ref[...] = update.astype(jnp.bfloat16).reshape(update_ref.shape)
            middles[...] = middle
            queries[...] = project(normal, query_ref[...]) * float(HEAD_DIM) ** (-0.5)
    group = lanes // seqs
    head_of = lax.broadcasted_iota(jnp.int32, (seq_dev, lanes), 1) // HEAD_DIM
    size = group * seqs
    row_column = lax.broadcasted_iota(jnp.int32, (group * HEADS * seq_dev, size), 0) // (
        HEADS * seq_dev
    )
    same = row_column == lax.broadcasted_iota(jnp.int32, row_column.shape, 1) // seqs
    ones = jnp.ones((size, lanes), jnp.bfloat16)
    for first in range(0, col_dev, group):
        query, key, value = [], [], []
        for column in range(first, first + group):
            row = queries[pl.ds(column, seq_dev, stride=col_dev), :]
            query += [jnp.where(head_of == head, row, 0.0) for head in range(HEADS)]
            key.append(keys[pl.ds(column, seqs, stride=col_dev), :])
            value.append(values[pl.ds(column, seqs, stride=col_dev), :])
        query, key, value = (
            jnp.concatenate(part, axis=0).astype(jnp.bfloat16) for part in (query, key, value)
        )
        scores = jnp.where(same, contract_last(query, key), -jnp.inf)
        weights = jnp.exp(scores - jnp.max(scores, axis=-1, keepdims=True))
        both = project(weights.astype(jnp.bfloat16), jnp.concatenate([value, ones], axis=1))
        for place in range(group):
            above = jnp.zeros((seq_dev, lanes), jnp.float32)
            below = jnp.ones((seq_dev, lanes), jnp.float32)
            for head in range(HEADS):
                at = (place * HEADS + head) * seq_dev
                above = jnp.where(head_of == head, both[at : at + seq_dev, :lanes], above)
                below = jnp.where(head_of == head, both[at : at + seq_dev, lanes:], below)
            contexts[pl.ds(first + place, seq_dev, stride=col_dev), :] = above / below
    layer = middles[...] + project(contexts[...].astype(jnp.bfloat16), output_ref[...])
    layer_ref[...] = layer.astype(jnp.bfloat16).reshape(layer_ref.shape)


def by_head(
    alignment,
    row_query,
    row_key,
    row_value,
    row_output,
    column_query,
    column_key,
    column_value,
    column_output,
):
    seq_dev, col_dev, width = alignment.shape
    inner = row_query.shape[1]
    seq, col = lax.axis_size("seq"), lax.axis_size("col")
    scale = float(HEAD_DIM * seq_dev * seq) ** (-0.5)
    bf16, f32 = jnp.bfloat16, jnp.float32
    vmem = pl.BlockSpec(memory_space=pltpu.VMEM)
    grant = pltpu.CompilerParams(vmem_limit_bytes=8 << 20)
    gate = pl.pallas_call(
        gate_kernel,
        out_shape=jax.ShapeDtypeStruct((8, inner), f32),
        out_specs=vmem,
        compiler_params=grant,
        cost_estimate=pl.CostEstimate(flops=1 << 33, transcendentals=0, bytes_accessed=1 << 24),
        name="gate",
    )()
    fields = {0: alignment}
    for place in range(seq - 1, 0, -1):
        fields[place] = lax.ppermute(alignment, "seq", [(i, i ^ place) for i in range(seq)])
    fields = [fields[place] for place in range(seq)]
    blocks = pl.pallas_call(
        project_kernel,
        out_shape=jax.ShapeDtypeStruct((seq, col // 2, 2, 2, col_dev, inner), bf16),
        in_specs=[vmem] * 4,
        out_specs=vmem,
        compiler_params=grant,
        name="project",
    )(alignment, row_key, row_value, gate)
    mine = lax.all_to_all(blocks.reshape(seq * col, 2, col_dev, inner), ("seq", "col"), 0, 0)
    other = lax.ppermute(mine, "col", [(i, i ^ 1) for i in range(col)])
    shape = (seq, col, 2, col_dev, inner)
    mine, other = mine.reshape(shape), other.reshape(shape)
    halves = seq_dev // HEADS
    queries = pl.pallas_call(
        query_kernel,
        out_shape=jax.ShapeDtypeStruct((halves, seq, col_dev, inner), bf16),
        in_specs=[vmem] * (seq + 1),
        out_specs=vmem,
        compiler_params=grant,
        name="query",
    )(*fields, row_query)
    parts = pl.pallas_call(
        functools.partial(attend_kernel, scale),
        out_shape=jax.ShapeDtypeStruct((seq, halves * seq, col_dev, inner), bf16),
        in_specs=[vmem] * 3,
        out_specs=vmem,
        compiler_params=grant,
        name="attend",
    )(mine, other, queries)
    parts = lax.all_to_all(parts, "seq", 0, 0)
    total = seq * seq_dev * col_dev
    local = seq_dev * col_dev
    like = jax.ShapeDtypeStruct(alignment.shape, bf16)
    return pl.pallas_call(
        finish_kernel,
        out_shape=(like, like),
        in_specs=[vmem] * (seq + 6),
        out_specs=(vmem, vmem),
        scratch_shapes=[
            pltpu.VMEM((local, width), f32),
            pltpu.VMEM((local, inner), f32),
            pltpu.VMEM((total, inner), f32),
            pltpu.VMEM((total, inner), f32),
            pltpu.VMEM((local, inner), f32),
        ],
        compiler_params=grant,
        name="finish",
    )(*fields, parts, row_output, column_query, column_key, column_value, column_output)


def suits_by_head(seq, col, seq_dev, col_dev, width, inner):
    return (
        seq == HEADS
        and col % 2 == 0
        and seq_dev == 2 * HEADS
        and col_dev % 16 == 0
        and inner == HEADS * HEAD_DIM
        and inner == 128
        and width % inner == 0
        and inner % (seq * seq_dev) == 0
        and col_dev % (inner // (seq * seq_dev)) == 0
        and seq * seq_dev * col_dev <= 1024
        and col * col_dev <= 512
    )


def solution(mesh):
    def choose(*args):
        seq_dev, col_dev, width = args[0].shape
        sizes = (mesh.shape["seq"], mesh.shape["col"], seq_dev, col_dev, width, args[1].shape[1])
        return (by_head if suits_by_head(*sizes) else on_device)(*args)

    return jax.shard_map(
        choose,
        mesh=mesh,
        in_specs=(P("seq", "col", None), P(), P(), P(), P(), P(), P(), P(), P()),
        out_specs=(P("seq", "col", None), P("seq", "col", None)),
        check_vma=False,
    )
```

```python
import functools

import jax
import jax.numpy as jnp
from jax import lax
from jax.experimental import pallas as pl
from jax.experimental.pallas import tpu as pltpu
from jax.sharding import PartitionSpec as P


HEADS = 4
HEAD_DIM = 32


def layer_norm(field):
    values = field.astype(jnp.float32)
    mean = jnp.mean(values, axis=-1, keepdims=True)
    centred = values - mean
    variance = jnp.mean(centred * centred, axis=-1, keepdims=True)
    return (centred * lax.rsqrt(variance + 1e-05)).astype(jnp.bfloat16)


def project(field, weight):
    return jnp.dot(field, weight, preferred_element_type=jnp.float32)


def gather(block, axis, groups=None, size=None):
    size = lax.axis_size(axis) if size is None else size
    copies = jnp.broadcast_to(block[None], (size,) + block.shape)
    return lax.all_to_all(copies, axis, 0, 0, axis_index_groups=groups)


def gather_columns(block):
    size = lax.axis_size("col")
    if size % 2 or size == 2:
        return gather(block, "col")
    groups = [[i for i in range(size) if i % 2 == parity] for parity in (0, 1)]
    mine = gather(block, "col", groups, size // 2)
    other = lax.ppermute(mine, "col", [(i, i ^ 1) for i in range(size)])
    return jnp.concatenate([mine, other], axis=0)


def column_attend(queries, keys, values):
    seq_rows, columns, inner = queries.shape
    query_heads = queries.reshape(seq_rows, columns, HEADS, HEAD_DIM)
    key_heads = keys.reshape(keys.shape[0], columns, HEADS, HEAD_DIM)
    value_heads = values.reshape(values.shape[0], columns, HEADS, HEAD_DIM)
    scores = jnp.einsum(
        "schd,tchd->chst", query_heads, key_heads, preferred_element_type=jnp.float32
    ) * float(HEAD_DIM) ** (-0.5)
    weights = jax.nn.softmax(scores, axis=-1).astype(jnp.bfloat16)
    context = jnp.einsum(
        "chst,tchd->schd", weights, value_heads, preferred_element_type=jnp.float32
    )
    return context.reshape(seq_rows, columns, inner).astype(jnp.bfloat16)


def on_device(
    alignment,
    row_query,
    row_key,
    row_value,
    row_output,
    column_query,
    column_key,
    column_value,
    column_output,
):
    seq_dev, col_dev, _ = alignment.shape
    inner = row_query.shape[1]
    scale = float(HEAD_DIM * seq_dev * lax.axis_size("seq")) ** (-0.5)
    normed = layer_norm(alignment)
    queries = project(normed, row_query).astype(jnp.bfloat16)
    key_value = project(normed, jnp.concatenate([row_key, row_value], axis=1)).astype(jnp.bfloat16)
    query_heads = queries.reshape(seq_dev, col_dev, HEADS, HEAD_DIM)
    every = gather_columns(key_value)
    key_heads = every[..., :inner].reshape(every.shape[0], seq_dev, col_dev, HEADS, HEAD_DIM)
    value_heads = every[..., inner:].reshape(every.shape[0], seq_dev, col_dev, HEADS, HEAD_DIM)
    partial_value = jnp.einsum(
        "sihd,gsjhd->higj", query_heads, key_heads, preferred_element_type=jnp.float32
    )
    shape = partial_value.shape
    partial_value = partial_value.reshape(shape[0], shape[1], -1)
    logits = jnp.sum(gather(partial_value, "seq"), axis=0) * scale
    probs = jax.nn.softmax(logits, axis=-1).astype(jnp.bfloat16).reshape(shape)
    context = jnp.einsum("higj,gsjhd->sihd", probs, value_heads, preferred_element_type=jnp.float32)
    context = context.reshape(seq_dev, col_dev, inner).astype(jnp.bfloat16)
    row_update = project(context, row_output).astype(jnp.bfloat16)
    middle = (alignment.astype(jnp.float32) + row_update.astype(jnp.float32)).astype(jnp.bfloat16)
    column_normed = layer_norm(middle)
    column_queries = project(column_normed, column_query).astype(jnp.bfloat16)
    column_pair = project(column_normed, jnp.concatenate([column_key, column_value], axis=1))
    every = gather(column_pair.astype(jnp.bfloat16), "seq")
    every = every.reshape((-1,) + every.shape[2:])
    column_context = column_attend(column_queries, every[..., :inner], every[..., inner:])
    layer_output = (middle.astype(jnp.float32) + project(column_context, column_output)).astype(
        jnp.bfloat16
    )
    return (row_update, layer_output)


def norm_rows(values):
    mean = jnp.mean(values, axis=-1, keepdims=True)
    centred = values - mean
    variance = jnp.mean(centred * centred, axis=-1, keepdims=True)
    return (centred * lax.rsqrt(variance + 1e-05)).astype(jnp.bfloat16)


def swap_groups(arrays, group):
    lanes = arrays[0].shape[-1]
    index = lax.broadcasted_iota(jnp.int32, arrays[0].shape, 1) // group
    arrays = list(arrays)
    step = len(arrays) // 2
    while step:
        low = (index // step) % 2 == 0
        for first in range(len(arrays)):
            if (first // step) % 2 == 0:
                one, two = arrays[first], arrays[first + step]
                shift = step * group
                arrays[first] = jnp.where(low, one, pltpu.roll(two, shift, 1))
                arrays[first + step] = jnp.where(low, pltpu.roll(one, lanes - shift, 1), two)
        step //= 2
    return arrays


def contract_last(left, right):
    return lax.dot_general(
        left, right, (((1,), (1,)), ((), ())), preferred_element_type=jnp.float32
    )


def gate_kernel(out_ref):
    out_ref[...] = jnp.zeros_like(out_ref)


def project_kernel(field_ref, key_ref, value_ref, gate_ref, out_ref):
    seq_dev, col_dev, width = field_ref.shape
    heads, chips, cores = out_ref.shape[:3]
    normed = norm_rows(field_ref[...].astype(jnp.float32).reshape(seq_dev * col_dev, width))
    for kind, weight_ref in enumerate((key_ref, value_ref)):
        rows = project(normed, weight_ref[...])
        for core in range(cores):
            first = core * heads
            tiles = [
                rows[(first + place) * col_dev : (first + place + 1) * col_dev]
                for place in range(heads)
            ]
            for head, tile in enumerate(swap_groups(tiles, HEAD_DIM)):
                tile = tile.astype(jnp.bfloat16)
                for chip in range(chips):
                    out_ref[head, chip, core, kind] = tile


def query_kernel(*refs):
    fields, (weight_ref, query_ref) = refs[:-2], refs[-2:]
    own = lax.axis_index("seq")
    seq_dev, col_dev, width = fields[0].shape
    seq, lanes = len(fields), weight_ref.shape[1]
    group = lax.broadcasted_iota(jnp.int32, weight_ref.shape, 1) // HEAD_DIM
    weight = weight_ref[...].astype(jnp.float32)
    spread = []
    for place in range(HEADS):
        shift = lax.rem((place + HEADS - own) * HEAD_DIM, lanes)
        spread.append(jnp.where(group == place, pltpu.roll(weight, shift, 1), 0.0))
    spread = jnp.concatenate(spread, axis=0).astype(jnp.bfloat16)
    normed = []
    for field_ref in fields:
        rows = norm_rows(field_ref[...].astype(jnp.float32).reshape(seq_dev * col_dev, width))
        for first in range(0, seq_dev, HEADS):
            normed.append(
                jnp.concatenate(
                    [
                        rows[place * col_dev : (place + 1) * col_dev]
                        for place in range(first, first + HEADS)
                    ],
                    axis=1,
                )
            )
    queries = project(jnp.concatenate(normed, axis=0), spread).astype(jnp.bfloat16)
    halves = seq_dev // HEADS
    for place in range(seq):
        for part in range(halves):
            start = (place * halves + part) * col_dev
            query_ref[part, own ^ place] = queries[start : start + col_dev]


def attend_kernel(scale, mine_ref, other_ref, query_ref, out_ref):
    half = lax.rem(lax.axis_index("col"), 2)
    seq, col, _, col_dev, lanes = mine_ref.shape
    logits = jnp.zeros((col_dev, col * col_dev), jnp.float32)
    for ref, part in ((mine_ref, half), (other_ref, 1 - half)):
        for source in range(seq):
            keys = ref[source, :, 0].reshape(col * col_dev, lanes)
            logits += contract_last(query_ref[part, source], keys)
    logits = logits * scale
    weights = jnp.exp(logits - jnp.max(logits, axis=-1, keepdims=True))
    probs = (weights / jnp.sum(weights, axis=-1, keepdims=True)).astype(jnp.bfloat16)
    for ref, part in ((mine_ref, half), (other_ref, 1 - half)):
        for source in range(seq):
            values = ref[source, :, 1].reshape(col * col_dev, lanes)
            out_ref[part * seq + source] = project(probs, values).astype(jnp.bfloat16)


def finish_kernel(*refs):
    tail = refs[-7:]
    refs, (row_output_ref, query_ref, key_ref, value_ref, output_ref) = refs[:-12], refs[-12:-7]
    fields, parts = refs[: len(refs) // 2], refs[len(refs) // 2 :]
    update_ref, layer_ref, middles, queries, keys, values, contexts = tail
    own = lax.axis_index("seq")
    seq = len(parts)
    _, col_dev, lanes = parts[0].shape
    seq_dev, _, width = update_ref.shape
    row_output = jnp.concatenate(
        [
            row_output_ref[pl.ds(pl.multiple_of((own ^ place) * HEAD_DIM, HEAD_DIM), HEAD_DIM), :]
            for place in range(HEADS)
        ],
        axis=0,
    )
    rows = seq_dev * col_dev
    seqs = seq * seq_dev
    pair = jnp.concatenate([key_ref[...], value_ref[...]], axis=1)
    for place, field_ref in enumerate(fields):
        source = own ^ place
        context = []
        for half in range(seq_dev // HEADS):
            heads = [part_ref[half * seq + source].astype(jnp.float32) for part_ref in parts]
            context += swap_groups(heads, HEAD_DIM)
        context = jnp.concatenate(context, axis=0).astype(jnp.bfloat16)
        update = project(context, row_output)
        middle = field_ref[...].reshape(rows, width).astype(jnp.float32) + update
        normal = norm_rows(middle)
        here = slice(place * rows, (place + 1) * rows)
        both = project(normal, pair)
        keys[here, :] = both[:, :lanes]
        values[here, :] = both[:, lanes:]
        if place == 0:
            update_ref[...] = update.astype(jnp.bfloat16).reshape(update_ref.shape)
            middles[...] = middle
            queries[...] = project(normal, query_ref[...]) * float(HEAD_DIM) ** (-0.5)
    group = lanes // seqs
    head_of = lax.broadcasted_iota(jnp.int32, (seq_dev, lanes), 1) // HEAD_DIM
    size = group * seqs
    row_column = lax.broadcasted_iota(jnp.int32, (group * HEADS * seq_dev, size), 0) // (
        HEADS * seq_dev
    )
    same = row_column == lax.broadcasted_iota(jnp.int32, row_column.shape, 1) // seqs
    ones = jnp.ones((size, lanes), jnp.bfloat16)
    for first in range(0, col_dev, group):
        query, key, value = [], [], []
        for column in range(first, first + group):
            row = queries[pl.ds(column, seq_dev, stride=col_dev), :]
            query += [jnp.where(head_of == head, row, 0.0) for head in range(HEADS)]
            key.append(keys[pl.ds(column, seqs, stride=col_dev), :])
            value.append(values[pl.ds(column, seqs, stride=col_dev), :])
        query, key, value = (
            jnp.concatenate(part, axis=0).astype(jnp.bfloat16) for part in (query, key, value)
        )
        scores = jnp.where(same, contract_last(query, key), -jnp.inf)
        weights = jnp.exp(scores - jnp.max(scores, axis=-1, keepdims=True))
        both = project(weights.astype(jnp.bfloat16), jnp.concatenate([value, ones], axis=1))
        for place in range(group):
            above = jnp.zeros((seq_dev, lanes), jnp.float32)
            below = jnp.ones((seq_dev, lanes), jnp.float32)
            for head in range(HEADS):
                at = (place * HEADS + head) * seq_dev
                above = jnp.where(head_of == head, both[at : at + seq_dev, :lanes], above)
                below = jnp.where(head_of == head, both[at : at + seq_dev, lanes:], below)
            contexts[pl.ds(first + place, seq_dev, stride=col_dev), :] = above / below
    layer = middles[...] + project(contexts[...].astype(jnp.bfloat16), output_ref[...])
    layer_ref[...] = layer.astype(jnp.bfloat16).reshape(layer_ref.shape)


def by_head(
    alignment,
    row_query,
    row_key,
    row_value,
    row_output,
    column_query,
    column_key,
    column_value,
    column_output,
):
    seq_dev, col_dev, width = alignment.shape
    inner = row_query.shape[1]
    seq, col = lax.axis_size("seq"), lax.axis_size("col")
    scale = float(HEAD_DIM * seq_dev * seq) ** (-0.5)
    bf16, f32 = jnp.bfloat16, jnp.float32
    vmem = pl.BlockSpec(memory_space=pltpu.VMEM)
    grant = pltpu.CompilerParams(vmem_limit_bytes=8 << 20)
    gate = pl.pallas_call(
        gate_kernel,
        out_shape=jax.ShapeDtypeStruct((8, inner), f32),
        out_specs=vmem,
        compiler_params=grant,
        cost_estimate=pl.CostEstimate(flops=1 << 33, transcendentals=0, bytes_accessed=1 << 24),
        name="gate",
    )()
    fields = {0: alignment}
    for place in range(seq - 1, 0, -1):
        fields[place] = lax.ppermute(alignment, "seq", [(i, i ^ place) for i in range(seq)])
    fields = [fields[place] for place in range(seq)]
    blocks = pl.pallas_call(
        project_kernel,
        out_shape=jax.ShapeDtypeStruct((seq, col // 2, 2, 2, col_dev, inner), bf16),
        in_specs=[vmem] * 4,
        out_specs=vmem,
        compiler_params=grant,
        name="project",
    )(alignment, row_key, row_value, gate)
    mine = lax.all_to_all(blocks.reshape(seq * col, 2, col_dev, inner), ("seq", "col"), 0, 0)
    other = lax.ppermute(mine, "col", [(i, i ^ 1) for i in range(col)])
    shape = (seq, col, 2, col_dev, inner)
    mine, other = mine.reshape(shape), other.reshape(shape)
    halves = seq_dev // HEADS
    queries = pl.pallas_call(
        query_kernel,
        out_shape=jax.ShapeDtypeStruct((halves, seq, col_dev, inner), bf16),
        in_specs=[vmem] * (seq + 1),
        out_specs=vmem,
        compiler_params=grant,
        name="query",
    )(*fields, row_query)
    parts = pl.pallas_call(
        functools.partial(attend_kernel, scale),
        out_shape=jax.ShapeDtypeStruct((halves * seq, col_dev, inner), bf16),
        in_specs=[vmem] * 3,
        out_specs=vmem,
        compiler_params=grant,
        name="attend",
    )(mine, other, queries)
    parts = [parts] * seq
    for place in range(seq - 1, 0, -1):
        parts[place] = lax.ppermute(parts[place], "seq", [(i, i ^ place) for i in range(seq)])
    total = seq * seq_dev * col_dev
    local = seq_dev * col_dev
    like = jax.ShapeDtypeStruct(alignment.shape, bf16)
    return pl.pallas_call(
        finish_kernel,
        out_shape=(like, like),
        in_specs=[vmem] * (2 * seq + 5),
        out_specs=(vmem, vmem),
        scratch_shapes=[
            pltpu.VMEM((local, width), f32),
            pltpu.VMEM((local, inner), f32),
            pltpu.VMEM((total, inner), f32),
            pltpu.VMEM((total, inner), f32),
            pltpu.VMEM((local, inner), f32),
        ],
        compiler_params=grant,
        name="finish",
    )(*fields, *parts, row_output, column_query, column_key, column_value, column_output)


def suits_by_head(seq, col, seq_dev, col_dev, width, inner):
    return (
        seq == HEADS
        and col % 2 == 0
        and seq_dev == 2 * HEADS
        and col_dev % 16 == 0
        and inner == HEADS * HEAD_DIM
        and inner == 128
        and width % inner == 0
        and inner % (seq * seq_dev) == 0
        and col_dev % (inner // (seq * seq_dev)) == 0
        and seq * seq_dev * col_dev <= 1024
        and col * col_dev <= 512
    )


def solution(mesh):
    def choose(*args):
        seq_dev, col_dev, width = args[0].shape
        sizes = (mesh.shape["seq"], mesh.shape["col"], seq_dev, col_dev, width, args[1].shape[1])
        return (by_head if suits_by_head(*sizes) else on_device)(*args)

    return jax.shard_map(
        choose,
        mesh=mesh,
        in_specs=(P("seq", "col", None), P(), P(), P(), P(), P(), P(), P(), P()),
        out_specs=(P("seq", "col", None), P("seq", "col", None)),
        check_vma=False,
    )
```

```python
import functools

import jax
import jax.numpy as jnp
from jax import lax
from jax.experimental import pallas as pl
from jax.experimental.pallas import tpu as pltpu
from jax.sharding import PartitionSpec as P


HEADS = 4
HEAD_DIM = 32


def layer_norm(field):
    values = field.astype(jnp.float32)
    mean = jnp.mean(values, axis=-1, keepdims=True)
    centred = values - mean
    variance = jnp.mean(centred * centred, axis=-1, keepdims=True)
    return (centred * lax.rsqrt(variance + 1e-05)).astype(jnp.bfloat16)


def project(field, weight):
    return jnp.dot(field, weight, preferred_element_type=jnp.float32)


def gather(block, axis, groups=None, size=None):
    size = lax.axis_size(axis) if size is None else size
    copies = jnp.broadcast_to(block[None], (size,) + block.shape)
    return lax.all_to_all(copies, axis, 0, 0, axis_index_groups=groups)


def gather_columns(block):
    size = lax.axis_size("col")
    if size % 2 or size == 2:
        return gather(block, "col")
    groups = [[i for i in range(size) if i % 2 == parity] for parity in (0, 1)]
    mine = gather(block, "col", groups, size // 2)
    other = lax.ppermute(mine, "col", [(i, i ^ 1) for i in range(size)])
    return jnp.concatenate([mine, other], axis=0)


def column_attend(queries, keys, values):
    seq_rows, columns, inner = queries.shape
    query_heads = queries.reshape(seq_rows, columns, HEADS, HEAD_DIM)
    key_heads = keys.reshape(keys.shape[0], columns, HEADS, HEAD_DIM)
    value_heads = values.reshape(values.shape[0], columns, HEADS, HEAD_DIM)
    scores = jnp.einsum(
        "schd,tchd->chst", query_heads, key_heads, preferred_element_type=jnp.float32
    ) * float(HEAD_DIM) ** (-0.5)
    weights = jax.nn.softmax(scores, axis=-1).astype(jnp.bfloat16)
    context = jnp.einsum(
        "chst,tchd->schd", weights, value_heads, preferred_element_type=jnp.float32
    )
    return context.reshape(seq_rows, columns, inner).astype(jnp.bfloat16)


def on_device(
    alignment,
    row_query,
    row_key,
    row_value,
    row_output,
    column_query,
    column_key,
    column_value,
    column_output,
):
    seq_dev, col_dev, _ = alignment.shape
    inner = row_query.shape[1]
    scale = float(HEAD_DIM * seq_dev * lax.axis_size("seq")) ** (-0.5)
    normed = layer_norm(alignment)
    queries = project(normed, row_query).astype(jnp.bfloat16)
    key_value = project(normed, jnp.concatenate([row_key, row_value], axis=1)).astype(jnp.bfloat16)
    query_heads = queries.reshape(seq_dev, col_dev, HEADS, HEAD_DIM)
    every = gather_columns(key_value)
    key_heads = every[..., :inner].reshape(every.shape[0], seq_dev, col_dev, HEADS, HEAD_DIM)
    value_heads = every[..., inner:].reshape(every.shape[0], seq_dev, col_dev, HEADS, HEAD_DIM)
    partial_value = jnp.einsum(
        "sihd,gsjhd->higj", query_heads, key_heads, preferred_element_type=jnp.float32
    )
    shape = partial_value.shape
    partial_value = partial_value.reshape(shape[0], shape[1], -1)
    logits = jnp.sum(gather(partial_value, "seq"), axis=0) * scale
    probs = jax.nn.softmax(logits, axis=-1).astype(jnp.bfloat16).reshape(shape)
    context = jnp.einsum("higj,gsjhd->sihd", probs, value_heads, preferred_element_type=jnp.float32)
    context = context.reshape(seq_dev, col_dev, inner).astype(jnp.bfloat16)
    row_update = project(context, row_output).astype(jnp.bfloat16)
    middle = (alignment.astype(jnp.float32) + row_update.astype(jnp.float32)).astype(jnp.bfloat16)
    column_normed = layer_norm(middle)
    column_queries = project(column_normed, column_query).astype(jnp.bfloat16)
    column_pair = project(column_normed, jnp.concatenate([column_key, column_value], axis=1))
    every = gather(column_pair.astype(jnp.bfloat16), "seq")
    every = every.reshape((-1,) + every.shape[2:])
    column_context = column_attend(column_queries, every[..., :inner], every[..., inner:])
    layer_output = (middle.astype(jnp.float32) + project(column_context, column_output)).astype(
        jnp.bfloat16
    )
    return (row_update, layer_output)


def norm_rows(values):
    mean = jnp.mean(values, axis=-1, keepdims=True)
    centred = values - mean
    variance = jnp.mean(centred * centred, axis=-1, keepdims=True)
    return (centred * lax.rsqrt(variance + 1e-05)).astype(jnp.bfloat16)


def swap_groups(arrays, group):
    lanes = arrays[0].shape[-1]
    index = lax.broadcasted_iota(jnp.int32, arrays[0].shape, 1) // group
    arrays = list(arrays)
    step = len(arrays) // 2
    while step:
        low = (index // step) % 2 == 0
        for first in range(len(arrays)):
            if (first // step) % 2 == 0:
                one, two = arrays[first], arrays[first + step]
                shift = step * group
                arrays[first] = jnp.where(low, one, pltpu.roll(two, shift, 1))
                arrays[first + step] = jnp.where(low, pltpu.roll(one, lanes - shift, 1), two)
        step //= 2
    return arrays


def contract_last(left, right):
    return lax.dot_general(
        left, right, (((1,), (1,)), ((), ())), preferred_element_type=jnp.float32
    )


def gate_kernel(out_ref):
    out_ref[...] = jnp.zeros_like(out_ref)


def project_kernel(field_ref, key_ref, value_ref, gate_ref, out_ref):
    seq_dev, col_dev, width = field_ref.shape
    heads, chips, cores = out_ref.shape[:3]
    normed = norm_rows(field_ref[...].astype(jnp.float32).reshape(seq_dev * col_dev, width))
    for kind, weight_ref in enumerate((key_ref, value_ref)):
        rows = project(normed, weight_ref[...])
        for core in range(cores):
            first = core * heads
            tiles = [
                rows[(first + place) * col_dev : (first + place + 1) * col_dev]
                for place in range(heads)
            ]
            for head, tile in enumerate(swap_groups(tiles, HEAD_DIM)):
                tile = tile.astype(jnp.bfloat16)
                for chip in range(chips):
                    out_ref[head, chip, core, kind] = tile


def query_kernel(*refs):
    fields, (weight_ref, query_ref) = refs[:-2], refs[-2:]
    own = lax.axis_index("seq")
    seq_dev, col_dev, width = fields[0].shape
    seq, lanes = len(fields), weight_ref.shape[1]
    group = lax.broadcasted_iota(jnp.int32, weight_ref.shape, 1) // HEAD_DIM
    weight = weight_ref[...].astype(jnp.float32)
    spread = []
    for place in range(HEADS):
        shift = lax.rem((place + HEADS - own) * HEAD_DIM, lanes)
        spread.append(jnp.where(group == place, pltpu.roll(weight, shift, 1), 0.0))
    spread = jnp.concatenate(spread, axis=0).astype(jnp.bfloat16)
    normed = []
    for field_ref in fields:
        rows = norm_rows(field_ref[...].astype(jnp.float32).reshape(seq_dev * col_dev, width))
        for first in range(0, seq_dev, HEADS):
            normed.append(
                jnp.concatenate(
                    [
                        rows[place * col_dev : (place + 1) * col_dev]
                        for place in range(first, first + HEADS)
                    ],
                    axis=1,
                )
            )
    queries = project(jnp.concatenate(normed, axis=0), spread).astype(jnp.bfloat16)
    halves = seq_dev // HEADS
    for place in range(seq):
        for part in range(halves):
            start = (place * halves + part) * col_dev
            query_ref[part, own ^ place] = queries[start : start + col_dev]


def half_logits(ref, query_ref, part):
    seq, col, _, col_dev, lanes = ref.shape
    logits = jnp.zeros((col_dev, col * col_dev), jnp.float32)
    for source in range(seq):
        keys = ref[source, :, 0].reshape(col * col_dev, lanes)
        logits += contract_last(query_ref[part, source], keys)
    return logits


def half_kernel(mine_ref, query_ref, logits_ref):
    half = lax.rem(lax.axis_index("col"), 2)
    logits_ref[...] = half_logits(mine_ref, query_ref, half)


def attend_kernel(scale, mine_ref, other_ref, query_ref, logits_ref, out_ref):
    half = lax.rem(lax.axis_index("col"), 2)
    seq, col, _, col_dev, lanes = mine_ref.shape
    logits = logits_ref[...] + half_logits(other_ref, query_ref, 1 - half)
    logits = logits * scale
    weights = jnp.exp(logits - jnp.max(logits, axis=-1, keepdims=True))
    probs = (weights / jnp.sum(weights, axis=-1, keepdims=True)).astype(jnp.bfloat16)
    for ref, part in ((mine_ref, half), (other_ref, 1 - half)):
        for source in range(seq):
            values = ref[source, :, 1].reshape(col * col_dev, lanes)
            out_ref[part * seq + source] = project(probs, values).astype(jnp.bfloat16)


def finish_kernel(*refs):
    tail = refs[-3:]
    refs, (row_output_ref, query_ref, key_ref, value_ref, output_ref) = refs[:-8], refs[-8:-3]
    fields, parts = refs[: len(refs) // 2], refs[len(refs) // 2 :]
    update_ref, layer_ref, middles = tail
    own = lax.axis_index("seq")
    seq = len(parts)
    _, col_dev, lanes = parts[0].shape
    seq_dev, _, width = update_ref.shape
    row_output = jnp.concatenate(
        [
            row_output_ref[pl.ds(pl.multiple_of((own ^ place) * HEAD_DIM, HEAD_DIM), HEAD_DIM), :]
            for place in range(HEADS)
        ],
        axis=0,
    )
    rows = seq_dev * col_dev
    seqs = seq * seq_dev
    pair = jnp.concatenate([key_ref[...], value_ref[...]], axis=1)
    context = []
    for place in range(seq):
        for half in range(seq_dev // HEADS):
            tile = half * seq + (own ^ place)
            context += swap_groups(
                [part_ref[tile].astype(jnp.float32) for part_ref in parts], HEAD_DIM
            )
    context = jnp.concatenate(context, axis=0).astype(jnp.bfloat16)
    update = project(context, row_output)
    update_ref[...] = update[:rows].astype(jnp.bfloat16).reshape(update_ref.shape)
    for place, field_ref in enumerate(fields):
        here = slice(place * rows, (place + 1) * rows)
        field = field_ref[...].reshape(rows, width).astype(jnp.float32)
        middles[here, :] = field + update[here]
    normal = norm_rows(middles[...])
    step = 8
    both = project(normal, pair).reshape(seqs, col_dev, 2 * lanes)
    queries = project(normal[:rows], query_ref[...]) * float(HEAD_DIM) ** (-0.5)
    queries = queries.reshape(seq_dev, col_dev, lanes)
    size = HEADS * seq_dev * step
    head_of = lax.broadcasted_iota(jnp.int32, (seq_dev * step, lanes), 1) // HEAD_DIM
    same = (
        lax.broadcasted_iota(jnp.int32, (size, seqs * step), 0) % step
        == lax.broadcasted_iota(jnp.int32, (size, seqs * step), 1) % step
    )
    ones = jnp.ones((seqs * step, lanes), jnp.bfloat16)
    contexts = []
    for first in range(0, col_dev, step):
        row = queries[:, first : first + step].reshape(seq_dev * step, lanes)
        query = jnp.concatenate(
            [jnp.where(head_of == head, row, 0.0) for head in range(HEADS)], axis=0
        ).astype(jnp.bfloat16)
        part = both[:, first : first + step].reshape(seqs * step, 2 * lanes).astype(jnp.bfloat16)
        scores = jnp.where(same, contract_last(query, part[:, :lanes]), -jnp.inf)
        weights = jnp.exp(scores - jnp.max(scores, axis=-1, keepdims=True)).astype(jnp.bfloat16)
        sums = project(weights, jnp.concatenate([part[:, lanes:], ones], axis=1))
        above = sums[: seq_dev * step, :lanes]
        below = sums[: seq_dev * step, lanes:]
        for head in range(1, HEADS):
            here = slice(head * seq_dev * step, (head + 1) * seq_dev * step)
            above = jnp.where(head_of == head, sums[here, :lanes], above)
            below = jnp.where(head_of == head, sums[here, lanes:], below)
        contexts.append((above / below).reshape(seq_dev, step, lanes))
    context = jnp.concatenate(contexts, axis=1).reshape(rows, lanes).astype(jnp.bfloat16)
    layer = middles[:rows, :] + project(context, output_ref[...])
    layer_ref[...] = layer.astype(jnp.bfloat16).reshape(layer_ref.shape)


def by_head(
    alignment,
    row_query,
    row_key,
    row_value,
    row_output,
    column_query,
    column_key,
    column_value,
    column_output,
):
    seq_dev, col_dev, width = alignment.shape
    inner = row_query.shape[1]
    seq, col = lax.axis_size("seq"), lax.axis_size("col")
    scale = float(HEAD_DIM * seq_dev * seq) ** (-0.5)
    bf16, f32 = jnp.bfloat16, jnp.float32
    vmem = pl.BlockSpec(memory_space=pltpu.VMEM)
    grant = pltpu.CompilerParams(vmem_limit_bytes=8 << 20)
    gate = pl.pallas_call(
        gate_kernel,
        out_shape=jax.ShapeDtypeStruct((8, inner), f32),
        out_specs=vmem,
        compiler_params=grant,
        cost_estimate=pl.CostEstimate(flops=1 << 33, transcendentals=0, bytes_accessed=1 << 24),
        name="gate",
    )()
    fields = {0: alignment}
    for place in range(seq - 1, 0, -1):
        fields[place] = lax.ppermute(alignment, "seq", [(i, i ^ place) for i in range(seq)])
    fields = [fields[place] for place in range(seq)]
    blocks = pl.pallas_call(
        project_kernel,
        out_shape=jax.ShapeDtypeStruct((seq, col // 2, 2, 2, col_dev, inner), bf16),
        in_specs=[vmem] * 4,
        out_specs=vmem,
        compiler_params=grant,
        name="project",
    )(alignment, row_key, row_value, gate)
    mine = lax.all_to_all(blocks.reshape(seq * col, 2, col_dev, inner), ("seq", "col"), 0, 0)
    other = lax.ppermute(mine, "col", [(i, i ^ 1) for i in range(col)])
    shape = (seq, col, 2, col_dev, inner)
    mine, other = mine.reshape(shape), other.reshape(shape)
    halves = seq_dev // HEADS
    queries = pl.pallas_call(
        query_kernel,
        out_shape=jax.ShapeDtypeStruct((halves, seq, col_dev, inner), bf16),
        in_specs=[vmem] * (seq + 1),
        out_specs=vmem,
        compiler_params=grant,
        name="query",
    )(*fields, row_query)
    logits = pl.pallas_call(
        half_kernel,
        out_shape=jax.ShapeDtypeStruct((col_dev, col * col_dev), f32),
        in_specs=[vmem] * 2,
        out_specs=vmem,
        compiler_params=grant,
        name="half",
    )(mine, queries)
    parts = pl.pallas_call(
        functools.partial(attend_kernel, scale),
        out_shape=jax.ShapeDtypeStruct((halves * seq, col_dev, inner), bf16),
        in_specs=[vmem] * 4,
        out_specs=vmem,
        compiler_params=grant,
        name="attend",
    )(mine, other, queries, logits)
    parts = [parts] * seq
    for place in range(seq - 1, 0, -1):
        parts[place] = lax.ppermute(parts[place], "seq", [(i, i ^ place) for i in range(seq)])
    total = seq * seq_dev * col_dev
    like = jax.ShapeDtypeStruct(alignment.shape, bf16)
    return pl.pallas_call(
        finish_kernel,
        out_shape=(like, like),
        in_specs=[vmem] * (2 * seq + 5),
        out_specs=(vmem, vmem),
        scratch_shapes=[
            pltpu.VMEM((total, width), f32),
        ],
        compiler_params=grant,
        name="finish",
    )(*fields, *parts, row_output, column_query, column_key, column_value, column_output)


def suits_by_head(seq, col, seq_dev, col_dev, width, inner):
    return (
        seq == HEADS
        and col % 2 == 0
        and seq_dev == 2 * HEADS
        and col_dev % 16 == 0
        and inner == HEADS * HEAD_DIM
        and inner == 128
        and width % inner == 0
        and inner % (seq * seq_dev) == 0
        and col_dev % (inner // (seq * seq_dev)) == 0
        and seq * seq_dev * col_dev <= 1024
        and col * col_dev <= 512
    )


def solution(mesh):
    def choose(*args):
        seq_dev, col_dev, width = args[0].shape
        sizes = (mesh.shape["seq"], mesh.shape["col"], seq_dev, col_dev, width, args[1].shape[1])
        return (by_head if suits_by_head(*sizes) else on_device)(*args)

    return jax.shard_map(
        choose,
        mesh=mesh,
        in_specs=(P("seq", "col", None), P(), P(), P(), P(), P(), P(), P(), P()),
        out_specs=(P("seq", "col", None), P("seq", "col", None)),
        check_vma=False,
    )
```

```python
import functools

import jax
import jax.numpy as jnp
from jax import lax
from jax.experimental import pallas as pl
from jax.experimental.pallas import tpu as pltpu
from jax.sharding import PartitionSpec as P


HEADS = 4
HEAD_DIM = 32


def layer_norm(field):
    values = field.astype(jnp.float32)
    mean = jnp.mean(values, axis=-1, keepdims=True)
    centred = values - mean
    variance = jnp.mean(centred * centred, axis=-1, keepdims=True)
    return (centred * lax.rsqrt(variance + 1e-05)).astype(jnp.bfloat16)


def project(field, weight):
    return jnp.dot(field, weight, preferred_element_type=jnp.float32)


def gather(block, axis, groups=None, size=None):
    size = lax.axis_size(axis) if size is None else size
    copies = jnp.broadcast_to(block[None], (size,) + block.shape)
    return lax.all_to_all(copies, axis, 0, 0, axis_index_groups=groups)


def gather_columns(block):
    size = lax.axis_size("col")
    if size % 2 or size == 2:
        return gather(block, "col")
    groups = [[i for i in range(size) if i % 2 == parity] for parity in (0, 1)]
    mine = gather(block, "col", groups, size // 2)
    other = lax.ppermute(mine, "col", [(i, i ^ 1) for i in range(size)])
    return jnp.concatenate([mine, other], axis=0)


def column_attend(queries, keys, values):
    seq_rows, columns, inner = queries.shape
    query_heads = queries.reshape(seq_rows, columns, HEADS, HEAD_DIM)
    key_heads = keys.reshape(keys.shape[0], columns, HEADS, HEAD_DIM)
    value_heads = values.reshape(values.shape[0], columns, HEADS, HEAD_DIM)
    scores = jnp.einsum(
        "schd,tchd->chst", query_heads, key_heads, preferred_element_type=jnp.float32
    ) * float(HEAD_DIM) ** (-0.5)
    weights = jax.nn.softmax(scores, axis=-1).astype(jnp.bfloat16)
    context = jnp.einsum(
        "chst,tchd->schd", weights, value_heads, preferred_element_type=jnp.float32
    )
    return context.reshape(seq_rows, columns, inner).astype(jnp.bfloat16)


def on_device(
    alignment,
    row_query,
    row_key,
    row_value,
    row_output,
    column_query,
    column_key,
    column_value,
    column_output,
):
    seq_dev, col_dev, _ = alignment.shape
    inner = row_query.shape[1]
    scale = float(HEAD_DIM * seq_dev * lax.axis_size("seq")) ** (-0.5)
    normed = layer_norm(alignment)
    queries = project(normed, row_query).astype(jnp.bfloat16)
    key_value = project(normed, jnp.concatenate([row_key, row_value], axis=1)).astype(jnp.bfloat16)
    query_heads = queries.reshape(seq_dev, col_dev, HEADS, HEAD_DIM)
    every = gather_columns(key_value)
    key_heads = every[..., :inner].reshape(every.shape[0], seq_dev, col_dev, HEADS, HEAD_DIM)
    value_heads = every[..., inner:].reshape(every.shape[0], seq_dev, col_dev, HEADS, HEAD_DIM)
    partial_value = jnp.einsum(
        "sihd,gsjhd->higj", query_heads, key_heads, preferred_element_type=jnp.float32
    )
    shape = partial_value.shape
    partial_value = partial_value.reshape(shape[0], shape[1], -1)
    logits = jnp.sum(gather(partial_value, "seq"), axis=0) * scale
    probs = jax.nn.softmax(logits, axis=-1).astype(jnp.bfloat16).reshape(shape)
    context = jnp.einsum("higj,gsjhd->sihd", probs, value_heads, preferred_element_type=jnp.float32)
    context = context.reshape(seq_dev, col_dev, inner).astype(jnp.bfloat16)
    row_update = project(context, row_output).astype(jnp.bfloat16)
    middle = (alignment.astype(jnp.float32) + row_update.astype(jnp.float32)).astype(jnp.bfloat16)
    column_normed = layer_norm(middle)
    column_queries = project(column_normed, column_query).astype(jnp.bfloat16)
    column_pair = project(column_normed, jnp.concatenate([column_key, column_value], axis=1))
    every = gather(column_pair.astype(jnp.bfloat16), "seq")
    every = every.reshape((-1,) + every.shape[2:])
    column_context = column_attend(column_queries, every[..., :inner], every[..., inner:])
    layer_output = (middle.astype(jnp.float32) + project(column_context, column_output)).astype(
        jnp.bfloat16
    )
    return (row_update, layer_output)


def norm_rows(values):
    mean = jnp.mean(values, axis=-1, keepdims=True)
    centred = values - mean
    variance = jnp.mean(centred * centred, axis=-1, keepdims=True)
    return (centred * lax.rsqrt(variance + 1e-05)).astype(jnp.bfloat16)


def swap_groups(arrays, group):
    lanes = arrays[0].shape[-1]
    index = lax.broadcasted_iota(jnp.int32, arrays[0].shape, 1) // group
    arrays = list(arrays)
    step = len(arrays) // 2
    while step:
        low = (index // step) % 2 == 0
        for first in range(len(arrays)):
            if (first // step) % 2 == 0:
                one, two = arrays[first], arrays[first + step]
                shift = step * group
                arrays[first] = jnp.where(low, one, pltpu.roll(two, shift, 1))
                arrays[first + step] = jnp.where(low, pltpu.roll(one, lanes - shift, 1), two)
        step //= 2
    return arrays


def contract_last(left, right):
    return lax.dot_general(
        left, right, (((1,), (1,)), ((), ())), preferred_element_type=jnp.float32
    )


def gate_kernel(out_ref):
    out_ref[...] = jnp.zeros_like(out_ref)


def project_kernel(field_ref, key_ref, value_ref, gate_ref, out_ref):
    seq_dev, col_dev, width = field_ref.shape
    heads, chips, cores = out_ref.shape[:3]
    normed = norm_rows(field_ref[...].astype(jnp.float32).reshape(seq_dev * col_dev, width))
    for kind, weight_ref in enumerate((key_ref, value_ref)):
        rows = project(normed, weight_ref[...])
        for core in range(cores):
            first = core * heads
            tiles = [
                rows[(first + place) * col_dev : (first + place + 1) * col_dev]
                for place in range(heads)
            ]
            for head, tile in enumerate(swap_groups(tiles, HEAD_DIM)):
                tile = tile.astype(jnp.bfloat16)
                for chip in range(chips):
                    out_ref[head, chip, core, kind] = tile


def query_kernel(*refs):
    fields, (weight_ref, query_ref) = refs[:-2], refs[-2:]
    own = lax.axis_index("seq")
    seq_dev, col_dev, width = fields[0].shape
    seq, lanes = len(fields), weight_ref.shape[1]
    group = lax.broadcasted_iota(jnp.int32, weight_ref.shape, 1) // HEAD_DIM
    weight = weight_ref[...].astype(jnp.float32)
    spread = []
    for place in range(HEADS):
        shift = lax.rem((place + HEADS - own) * HEAD_DIM, lanes)
        spread.append(jnp.where(group == place, pltpu.roll(weight, shift, 1), 0.0))
    spread = jnp.concatenate(spread, axis=0).astype(jnp.bfloat16)
    normed = []
    for field_ref in fields:
        rows = norm_rows(field_ref[...].astype(jnp.float32).reshape(seq_dev * col_dev, width))
        for first in range(0, seq_dev, HEADS):
            normed.append(
                jnp.concatenate(
                    [
                        rows[place * col_dev : (place + 1) * col_dev]
                        for place in range(first, first + HEADS)
                    ],
                    axis=1,
                )
            )
    queries = project(jnp.concatenate(normed, axis=0), spread).astype(jnp.bfloat16)
    halves = seq_dev // HEADS
    for place in range(seq):
        for part in range(halves):
            start = (place * halves + part) * col_dev
            query_ref[part, own ^ place] = queries[start : start + col_dev]


def half_logits(ref, query_ref, part):
    seq, col, _, col_dev, lanes = ref.shape
    logits = jnp.zeros((col_dev, col * col_dev), jnp.float32)
    for first in range(0, seq, 2):
        both = range(first, first + 2)
        keys = [ref[source, :, 0].reshape(col * col_dev, lanes) for source in both]
        queries = [query_ref[part, source] for source in both]
        logits += contract_last(jnp.concatenate(queries, axis=1), jnp.concatenate(keys, axis=1))
    return logits


def half_kernel(mine_ref, query_ref, logits_ref):
    half = lax.rem(lax.axis_index("col"), 2)
    logits_ref[...] = half_logits(mine_ref, query_ref, half)


def attend_kernel(scale, mine_ref, other_ref, query_ref, logits_ref, out_ref):
    half = lax.rem(lax.axis_index("col"), 2)
    seq, col, _, col_dev, lanes = mine_ref.shape
    logits = logits_ref[...] + half_logits(other_ref, query_ref, 1 - half)
    logits = logits * scale
    weights = jnp.exp(logits - jnp.max(logits, axis=-1, keepdims=True))
    share = 1.0 / jnp.sum(weights, axis=-1, keepdims=True)
    weights = weights.astype(jnp.bfloat16)
    for ref, part in ((mine_ref, half), (other_ref, 1 - half)):
        for first in range(0, seq, 2):
            values = [
                ref[source, :, 1].reshape(col * col_dev, lanes) for source in (first, first + 1)
            ]
            context = project(weights, jnp.concatenate(values, axis=1)) * share
            out_ref[part * seq + first] = context[:, :lanes].astype(jnp.bfloat16)
            out_ref[part * seq + first + 1] = context[:, lanes:].astype(jnp.bfloat16)


def finish_kernel(*refs):
    tail = refs[-3:]
    refs, (row_output_ref, query_ref, key_ref, value_ref, output_ref) = refs[:-8], refs[-8:-3]
    fields, parts = refs[: len(refs) // 2], refs[len(refs) // 2 :]
    update_ref, layer_ref, middles = tail
    own = lax.axis_index("seq")
    seq = len(parts)
    _, col_dev, lanes = parts[0].shape
    seq_dev, _, width = update_ref.shape
    row_output = jnp.concatenate(
        [
            row_output_ref[pl.ds(pl.multiple_of((own ^ place) * HEAD_DIM, HEAD_DIM), HEAD_DIM), :]
            for place in range(HEADS)
        ],
        axis=0,
    )
    rows = seq_dev * col_dev
    seqs = seq * seq_dev
    pair = jnp.concatenate([key_ref[...], value_ref[...]], axis=1)
    context = []
    for place in range(seq):
        for half in range(seq_dev // HEADS):
            tile = half * seq + (own ^ place)
            context += swap_groups(
                [part_ref[tile].astype(jnp.float32) for part_ref in parts], HEAD_DIM
            )
    context = jnp.concatenate(context, axis=0).astype(jnp.bfloat16)
    update = project(context, row_output)
    update_ref[...] = update[:rows].astype(jnp.bfloat16).reshape(update_ref.shape)
    for place, field_ref in enumerate(fields):
        here = slice(place * rows, (place + 1) * rows)
        field = field_ref[...].reshape(rows, width).astype(jnp.float32)
        middles[here, :] = field + update[here]
    normal = norm_rows(middles[...])
    step = 8
    both = project(normal, pair).reshape(seqs, col_dev, 2 * lanes)
    queries = project(normal[:rows], query_ref[...]) * float(HEAD_DIM) ** (-0.5)
    queries = queries.reshape(seq_dev, col_dev, lanes)
    size = HEADS * seq_dev * step
    head_of = lax.broadcasted_iota(jnp.int32, (seq_dev * step, lanes), 1) // HEAD_DIM
    same = (
        lax.broadcasted_iota(jnp.int32, (size, seqs * step), 0) % step
        == lax.broadcasted_iota(jnp.int32, (size, seqs * step), 1) % step
    )
    ones = jnp.ones((seqs * step, lanes), jnp.bfloat16)
    contexts = []
    for first in range(0, col_dev, step):
        row = queries[:, first : first + step].reshape(seq_dev * step, lanes)
        query = jnp.concatenate(
            [jnp.where(head_of == head, row, 0.0) for head in range(HEADS)], axis=0
        ).astype(jnp.bfloat16)
        part = both[:, first : first + step].reshape(seqs * step, 2 * lanes).astype(jnp.bfloat16)
        scores = jnp.where(same, contract_last(query, part[:, :lanes]), -jnp.inf)
        weights = jnp.exp(scores - jnp.max(scores, axis=-1, keepdims=True)).astype(jnp.bfloat16)
        sums = project(weights, jnp.concatenate([part[:, lanes:], ones], axis=1))
        above = sums[: seq_dev * step, :lanes]
        below = sums[: seq_dev * step, lanes:]
        for head in range(1, HEADS):
            here = slice(head * seq_dev * step, (head + 1) * seq_dev * step)
            above = jnp.where(head_of == head, sums[here, :lanes], above)
            below = jnp.where(head_of == head, sums[here, lanes:], below)
        contexts.append((above / below).reshape(seq_dev, step, lanes))
    context = jnp.concatenate(contexts, axis=1).reshape(rows, lanes).astype(jnp.bfloat16)
    layer = middles[:rows, :] + project(context, output_ref[...])
    layer_ref[...] = layer.astype(jnp.bfloat16).reshape(layer_ref.shape)


def by_head(
    alignment,
    row_query,
    row_key,
    row_value,
    row_output,
    column_query,
    column_key,
    column_value,
    column_output,
):
    seq_dev, col_dev, width = alignment.shape
    inner = row_query.shape[1]
    seq, col = lax.axis_size("seq"), lax.axis_size("col")
    scale = float(HEAD_DIM * seq_dev * seq) ** (-0.5)
    bf16, f32 = jnp.bfloat16, jnp.float32
    vmem = pl.BlockSpec(memory_space=pltpu.VMEM)
    grant = pltpu.CompilerParams(vmem_limit_bytes=8 << 20)
    gate = pl.pallas_call(
        gate_kernel,
        out_shape=jax.ShapeDtypeStruct((8, inner), f32),
        out_specs=vmem,
        compiler_params=grant,
        cost_estimate=pl.CostEstimate(flops=1 << 33, transcendentals=0, bytes_accessed=1 << 24),
        name="gate",
    )()
    fields = {0: alignment}
    for place in range(seq - 1, 0, -1):
        fields[place] = lax.ppermute(alignment, "seq", [(i, i ^ place) for i in range(seq)])
    fields = [fields[place] for place in range(seq)]
    blocks = pl.pallas_call(
        project_kernel,
        out_shape=jax.ShapeDtypeStruct((seq, col // 2, 2, 2, col_dev, inner), bf16),
        in_specs=[vmem] * 4,
        out_specs=vmem,
        compiler_params=grant,
        name="project",
    )(alignment, row_key, row_value, gate)
    mine = lax.all_to_all(blocks.reshape(seq * col, 2, col_dev, inner), ("seq", "col"), 0, 0)
    other = lax.ppermute(mine, "col", [(i, i ^ 1) for i in range(col)])
    shape = (seq, col, 2, col_dev, inner)
    mine, other = mine.reshape(shape), other.reshape(shape)
    halves = seq_dev // HEADS
    queries = pl.pallas_call(
        query_kernel,
        out_shape=jax.ShapeDtypeStruct((halves, seq, col_dev, inner), bf16),
        in_specs=[vmem] * (seq + 1),
        out_specs=vmem,
        compiler_params=grant,
        name="query",
    )(*fields, row_query)
    logits = pl.pallas_call(
        half_kernel,
        out_shape=jax.ShapeDtypeStruct((col_dev, col * col_dev), f32),
        in_specs=[vmem] * 2,
        out_specs=vmem,
        compiler_params=grant,
        name="half",
    )(mine, queries)
    parts = pl.pallas_call(
        functools.partial(attend_kernel, scale),
        out_shape=jax.ShapeDtypeStruct((halves * seq, col_dev, inner), bf16),
        in_specs=[vmem] * 4,
        out_specs=vmem,
        compiler_params=grant,
        name="attend",
    )(mine, other, queries, logits)
    parts = [parts] * seq
    for place in range(seq - 1, 0, -1):
        parts[place] = lax.ppermute(parts[place], "seq", [(i, i ^ place) for i in range(seq)])
    total = seq * seq_dev * col_dev
    like = jax.ShapeDtypeStruct(alignment.shape, bf16)
    return pl.pallas_call(
        finish_kernel,
        out_shape=(like, like),
        in_specs=[vmem] * (2 * seq + 5),
        out_specs=(vmem, vmem),
        scratch_shapes=[
            pltpu.VMEM((total, width), f32),
        ],
        compiler_params=grant,
        name="finish",
    )(*fields, *parts, row_output, column_query, column_key, column_value, column_output)


def suits_by_head(seq, col, seq_dev, col_dev, width, inner):
    return (
        seq == HEADS
        and col % 2 == 0
        and seq_dev == 2 * HEADS
        and col_dev % 16 == 0
        and inner == HEADS * HEAD_DIM
        and inner == 128
        and width % inner == 0
        and inner % (seq * seq_dev) == 0
        and col_dev % (inner // (seq * seq_dev)) == 0
        and seq * seq_dev * col_dev <= 1024
        and col * col_dev <= 512
    )


def solution(mesh):
    def choose(*args):
        seq_dev, col_dev, width = args[0].shape
        sizes = (mesh.shape["seq"], mesh.shape["col"], seq_dev, col_dev, width, args[1].shape[1])
        return (by_head if suits_by_head(*sizes) else on_device)(*args)

    return jax.shard_map(
        choose,
        mesh=mesh,
        in_specs=(P("seq", "col", None), P(), P(), P(), P(), P(), P(), P(), P()),
        out_specs=(P("seq", "col", None), P("seq", "col", None)),
        check_vma=False,
    )
```

```python
import functools

import jax
import jax.numpy as jnp
from jax import lax
from jax.experimental import pallas as pl
from jax.experimental.pallas import tpu as pltpu
from jax.sharding import PartitionSpec as P


HEADS = 4
HEAD_DIM = 32


def layer_norm(field):
    values = field.astype(jnp.float32)
    mean = jnp.mean(values, axis=-1, keepdims=True)
    centred = values - mean
    variance = jnp.mean(centred * centred, axis=-1, keepdims=True)
    return (centred * lax.rsqrt(variance + 1e-05)).astype(jnp.bfloat16)


def project(field, weight):
    return jnp.dot(field, weight, preferred_element_type=jnp.float32)


def gather(block, axis, groups=None, size=None):
    size = lax.axis_size(axis) if size is None else size
    copies = jnp.broadcast_to(block[None], (size,) + block.shape)
    return lax.all_to_all(copies, axis, 0, 0, axis_index_groups=groups)


def gather_columns(block):
    size = lax.axis_size("col")
    if size % 2 or size == 2:
        return gather(block, "col")
    groups = [[i for i in range(size) if i % 2 == parity] for parity in (0, 1)]
    mine = gather(block, "col", groups, size // 2)
    other = lax.ppermute(mine, "col", [(i, i ^ 1) for i in range(size)])
    return jnp.concatenate([mine, other], axis=0)


def column_attend(queries, keys, values):
    seq_rows, columns, inner = queries.shape
    query_heads = queries.reshape(seq_rows, columns, HEADS, HEAD_DIM)
    key_heads = keys.reshape(keys.shape[0], columns, HEADS, HEAD_DIM)
    value_heads = values.reshape(values.shape[0], columns, HEADS, HEAD_DIM)
    scores = jnp.einsum(
        "schd,tchd->chst", query_heads, key_heads, preferred_element_type=jnp.float32
    ) * float(HEAD_DIM) ** (-0.5)
    weights = jax.nn.softmax(scores, axis=-1).astype(jnp.bfloat16)
    context = jnp.einsum(
        "chst,tchd->schd", weights, value_heads, preferred_element_type=jnp.float32
    )
    return context.reshape(seq_rows, columns, inner).astype(jnp.bfloat16)


def on_device(
    alignment,
    row_query,
    row_key,
    row_value,
    row_output,
    column_query,
    column_key,
    column_value,
    column_output,
):
    seq_dev, col_dev, _ = alignment.shape
    inner = row_query.shape[1]
    scale = float(HEAD_DIM * seq_dev * lax.axis_size("seq")) ** (-0.5)
    normed = layer_norm(alignment)
    queries = project(normed, row_query).astype(jnp.bfloat16)
    key_value = project(normed, jnp.concatenate([row_key, row_value], axis=1)).astype(jnp.bfloat16)
    query_heads = queries.reshape(seq_dev, col_dev, HEADS, HEAD_DIM)
    every = gather_columns(key_value)
    key_heads = every[..., :inner].reshape(every.shape[0], seq_dev, col_dev, HEADS, HEAD_DIM)
    value_heads = every[..., inner:].reshape(every.shape[0], seq_dev, col_dev, HEADS, HEAD_DIM)
    partial_value = jnp.einsum(
        "sihd,gsjhd->higj", query_heads, key_heads, preferred_element_type=jnp.float32
    )
    shape = partial_value.shape
    partial_value = partial_value.reshape(shape[0], shape[1], -1)
    logits = jnp.sum(gather(partial_value, "seq"), axis=0) * scale
    probs = jax.nn.softmax(logits, axis=-1).astype(jnp.bfloat16).reshape(shape)
    context = jnp.einsum("higj,gsjhd->sihd", probs, value_heads, preferred_element_type=jnp.float32)
    context = context.reshape(seq_dev, col_dev, inner).astype(jnp.bfloat16)
    row_update = project(context, row_output).astype(jnp.bfloat16)
    middle = (alignment.astype(jnp.float32) + row_update.astype(jnp.float32)).astype(jnp.bfloat16)
    column_normed = layer_norm(middle)
    column_queries = project(column_normed, column_query).astype(jnp.bfloat16)
    column_pair = project(column_normed, jnp.concatenate([column_key, column_value], axis=1))
    every = gather(column_pair.astype(jnp.bfloat16), "seq")
    every = every.reshape((-1,) + every.shape[2:])
    column_context = column_attend(column_queries, every[..., :inner], every[..., inner:])
    layer_output = (middle.astype(jnp.float32) + project(column_context, column_output)).astype(
        jnp.bfloat16
    )
    return (row_update, layer_output)


def norm_rows(values):
    mean = jnp.mean(values, axis=-1, keepdims=True)
    centred = values - mean
    variance = jnp.mean(centred * centred, axis=-1, keepdims=True)
    return (centred * lax.rsqrt(variance + 1e-05)).astype(jnp.bfloat16)


def swap_groups(arrays, group):
    lanes = arrays[0].shape[-1]
    index = lax.broadcasted_iota(jnp.int32, arrays[0].shape, 1) // group
    arrays = list(arrays)
    step = len(arrays) // 2
    while step:
        low = (index // step) % 2 == 0
        for first in range(len(arrays)):
            if (first // step) % 2 == 0:
                one, two = arrays[first], arrays[first + step]
                shift = step * group
                arrays[first] = jnp.where(low, one, pltpu.roll(two, shift, 1))
                arrays[first + step] = jnp.where(low, pltpu.roll(one, lanes - shift, 1), two)
        step //= 2
    return arrays


def contract_last(left, right):
    return lax.dot_general(
        left, right, (((1,), (1,)), ((), ())), preferred_element_type=jnp.float32
    )


def gate_kernel(out_ref):
    out_ref[...] = jnp.zeros_like(out_ref)


def project_kernel(field_ref, key_ref, value_ref, gate_ref, out_ref):
    seq_dev, col_dev, width = field_ref.shape
    heads, chips, cores = out_ref.shape[:3]
    normed = norm_rows(field_ref[...].astype(jnp.float32).reshape(seq_dev * col_dev, width))
    inner = key_ref.shape[1]
    pair = project(normed, jnp.concatenate([key_ref[...], value_ref[...]], axis=1))
    for kind in range(2):
        rows = pair[:, kind * inner : (kind + 1) * inner]
        for core in range(cores):
            first = core * heads
            tiles = [
                rows[(first + place) * col_dev : (first + place + 1) * col_dev]
                for place in range(heads)
            ]
            for head, tile in enumerate(swap_groups(tiles, HEAD_DIM)):
                tile = tile.astype(jnp.bfloat16)
                for chip in range(chips):
                    out_ref[head, chip, core, kind] = tile


def query_kernel(*refs):
    fields, (weight_ref, query_ref) = refs[:-2], refs[-2:]
    own = lax.axis_index("seq")
    seq_dev, col_dev, width = fields[0].shape
    seq, lanes = len(fields), weight_ref.shape[1]
    group = lax.broadcasted_iota(jnp.int32, weight_ref.shape, 1) // HEAD_DIM
    weight = weight_ref[...].astype(jnp.float32)
    spread = []
    for place in range(HEADS):
        shift = lax.rem((place + HEADS - own) * HEAD_DIM, lanes)
        spread.append(jnp.where(group == place, pltpu.roll(weight, shift, 1), 0.0))
    spread = jnp.concatenate(spread, axis=0).astype(jnp.bfloat16)
    normed = []
    for field_ref in fields:
        rows = norm_rows(field_ref[...].astype(jnp.float32).reshape(seq_dev * col_dev, width))
        for first in range(0, seq_dev, HEADS):
            normed.append(
                jnp.concatenate(
                    [
                        rows[place * col_dev : (place + 1) * col_dev]
                        for place in range(first, first + HEADS)
                    ],
                    axis=1,
                )
            )
    queries = project(jnp.concatenate(normed, axis=0), spread).astype(jnp.bfloat16)
    halves = seq_dev // HEADS
    for place in range(seq):
        for part in range(halves):
            start = (place * halves + part) * col_dev
            query_ref[part, own ^ place] = queries[start : start + col_dev]


def half_logits(ref, query_ref, part):
    seq, col, _, col_dev, lanes = ref.shape
    logits = jnp.zeros((col_dev, col * col_dev), jnp.float32)
    for first in range(0, seq, 2):
        both = range(first, first + 2)
        keys = [ref[source, :, 0].reshape(col * col_dev, lanes) for source in both]
        queries = [query_ref[part, source] for source in both]
        logits += contract_last(jnp.concatenate(queries, axis=1), jnp.concatenate(keys, axis=1))
    return logits


def half_kernel(mine_ref, query_ref, logits_ref):
    half = lax.rem(lax.axis_index("col"), 2)
    logits_ref[...] = half_logits(mine_ref, query_ref, half)


def attend_kernel(scale, mine_ref, other_ref, query_ref, logits_ref, out_ref):
    half = lax.rem(lax.axis_index("col"), 2)
    seq, col, _, col_dev, lanes = mine_ref.shape
    logits = logits_ref[...] + half_logits(other_ref, query_ref, 1 - half)
    logits = logits * scale
    weights = jnp.exp(logits - jnp.max(logits, axis=-1, keepdims=True))
    share = 1.0 / jnp.sum(weights, axis=-1, keepdims=True)
    weights = weights.astype(jnp.bfloat16)
    for ref, part in ((mine_ref, half), (other_ref, 1 - half)):
        for first in range(0, seq, 2):
            values = [
                ref[source, :, 1].reshape(col * col_dev, lanes) for source in (first, first + 1)
            ]
            context = project(weights, jnp.concatenate(values, axis=1)) * share
            out_ref[part * seq + first] = context[:, :lanes].astype(jnp.bfloat16)
            out_ref[part * seq + first + 1] = context[:, lanes:].astype(jnp.bfloat16)


def finish_kernel(*refs):
    tail = refs[-3:]
    refs, (row_output_ref, query_ref, key_ref, value_ref, output_ref) = refs[:-8], refs[-8:-3]
    fields, parts = refs[: len(refs) // 2], refs[len(refs) // 2 :]
    update_ref, layer_ref, middles = tail
    own = lax.axis_index("seq")
    seq = len(parts)
    _, col_dev, lanes = parts[0].shape
    seq_dev, _, width = update_ref.shape
    row_output = jnp.concatenate(
        [
            row_output_ref[pl.ds(pl.multiple_of((own ^ place) * HEAD_DIM, HEAD_DIM), HEAD_DIM), :]
            for place in range(HEADS)
        ],
        axis=0,
    )
    rows = seq_dev * col_dev
    seqs = seq * seq_dev
    pair = jnp.concatenate([key_ref[...], value_ref[...]], axis=1)
    context = []
    for place in range(seq):
        for half in range(seq_dev // HEADS):
            tile = half * seq + (own ^ place)
            context += swap_groups(
                [part_ref[tile].astype(jnp.float32) for part_ref in parts], HEAD_DIM
            )
    context = jnp.concatenate(context, axis=0).astype(jnp.bfloat16)
    update = project(context, row_output)
    update_ref[...] = update[:rows].astype(jnp.bfloat16).reshape(update_ref.shape)
    for place, field_ref in enumerate(fields):
        here = slice(place * rows, (place + 1) * rows)
        field = field_ref[...].reshape(rows, width).astype(jnp.float32)
        middles[here, :] = field + update[here]
    normal = norm_rows(middles[...])
    step = 8
    both = project(normal, pair).reshape(seqs, col_dev, 2 * lanes)
    queries = project(normal[:rows], query_ref[...]) * float(HEAD_DIM) ** (-0.5)
    queries = queries.reshape(seq_dev, col_dev, lanes)
    size = HEADS * seq_dev * step
    head_of = lax.broadcasted_iota(jnp.int32, (seq_dev * step, lanes), 1) // HEAD_DIM
    same = (
        lax.broadcasted_iota(jnp.int32, (size, seqs * step), 0) % step
        == lax.broadcasted_iota(jnp.int32, (size, seqs * step), 1) % step
    )
    ones = jnp.ones((seqs * step, lanes), jnp.bfloat16)
    contexts = []
    for first in range(0, col_dev, step):
        row = queries[:, first : first + step].reshape(seq_dev * step, lanes)
        query = jnp.concatenate(
            [jnp.where(head_of == head, row, 0.0) for head in range(HEADS)], axis=0
        ).astype(jnp.bfloat16)
        part = both[:, first : first + step].reshape(seqs * step, 2 * lanes).astype(jnp.bfloat16)
        scores = jnp.where(same, contract_last(query, part[:, :lanes]), -jnp.inf)
        weights = jnp.exp(scores - jnp.max(scores, axis=-1, keepdims=True)).astype(jnp.bfloat16)
        sums = project(weights, jnp.concatenate([part[:, lanes:], ones], axis=1))
        above = sums[: seq_dev * step, :lanes]
        below = sums[: seq_dev * step, lanes:]
        for head in range(1, HEADS):
            here = slice(head * seq_dev * step, (head + 1) * seq_dev * step)
            above = jnp.where(head_of == head, sums[here, :lanes], above)
            below = jnp.where(head_of == head, sums[here, lanes:], below)
        contexts.append((above / below).reshape(seq_dev, step, lanes))
    context = jnp.concatenate(contexts, axis=1).reshape(rows, lanes).astype(jnp.bfloat16)
    layer = middles[:rows, :] + project(context, output_ref[...])
    layer_ref[...] = layer.astype(jnp.bfloat16).reshape(layer_ref.shape)


def by_head(
    alignment,
    row_query,
    row_key,
    row_value,
    row_output,
    column_query,
    column_key,
    column_value,
    column_output,
):
    seq_dev, col_dev, width = alignment.shape
    inner = row_query.shape[1]
    seq, col = lax.axis_size("seq"), lax.axis_size("col")
    scale = float(HEAD_DIM * seq_dev * seq) ** (-0.5)
    bf16, f32 = jnp.bfloat16, jnp.float32
    vmem = pl.BlockSpec(memory_space=pltpu.VMEM)
    grant = pltpu.CompilerParams(vmem_limit_bytes=8 << 20)
    gate = pl.pallas_call(
        gate_kernel,
        out_shape=jax.ShapeDtypeStruct((8, inner), f32),
        out_specs=vmem,
        compiler_params=grant,
        cost_estimate=pl.CostEstimate(flops=1 << 33, transcendentals=0, bytes_accessed=1 << 24),
        name="gate",
    )()
    fields = {0: alignment}
    for place in range(seq - 1, 0, -1):
        fields[place] = lax.ppermute(alignment, "seq", [(i, i ^ place) for i in range(seq)])
    fields = [fields[place] for place in range(seq)]
    blocks = pl.pallas_call(
        project_kernel,
        out_shape=jax.ShapeDtypeStruct((seq, col // 2, 2, 2, col_dev, inner), bf16),
        in_specs=[vmem] * 4,
        out_specs=vmem,
        compiler_params=grant,
        name="project",
    )(alignment, row_key, row_value, gate)
    mine = lax.all_to_all(blocks.reshape(seq * col, 2, col_dev, inner), ("seq", "col"), 0, 0)
    other = lax.ppermute(mine, "col", [(i, i ^ 1) for i in range(col)])
    shape = (seq, col, 2, col_dev, inner)
    mine, other = mine.reshape(shape), other.reshape(shape)
    halves = seq_dev // HEADS
    queries = pl.pallas_call(
        query_kernel,
        out_shape=jax.ShapeDtypeStruct((halves, seq, col_dev, inner), bf16),
        in_specs=[vmem] * (seq + 1),
        out_specs=vmem,
        compiler_params=grant,
        name="query",
    )(*fields, row_query)
    logits = pl.pallas_call(
        half_kernel,
        out_shape=jax.ShapeDtypeStruct((col_dev, col * col_dev), f32),
        in_specs=[vmem] * 2,
        out_specs=vmem,
        compiler_params=grant,
        name="half",
    )(mine, queries)
    parts = pl.pallas_call(
        functools.partial(attend_kernel, scale),
        out_shape=jax.ShapeDtypeStruct((halves * seq, col_dev, inner), bf16),
        in_specs=[vmem] * 4,
        out_specs=vmem,
        compiler_params=grant,
        name="attend",
    )(mine, other, queries, logits)
    parts = [parts] * seq
    for place in range(seq - 1, 0, -1):
        parts[place] = lax.ppermute(parts[place], "seq", [(i, i ^ place) for i in range(seq)])
    total = seq * seq_dev * col_dev
    like = jax.ShapeDtypeStruct(alignment.shape, bf16)
    return pl.pallas_call(
        finish_kernel,
        out_shape=(like, like),
        in_specs=[vmem] * (2 * seq + 5),
        out_specs=(vmem, vmem),
        scratch_shapes=[
            pltpu.VMEM((total, width), f32),
        ],
        compiler_params=pltpu.CompilerParams(vmem_limit_bytes=8 << 20),
        name="finish",
    )(*fields, *parts, row_output, column_query, column_key, column_value, column_output)


def suits_by_head(seq, col, seq_dev, col_dev, width, inner):
    return (
        seq == HEADS
        and col % 2 == 0
        and seq_dev == 2 * HEADS
        and col_dev % 16 == 0
        and inner == HEADS * HEAD_DIM
        and inner == 128
        and width % inner == 0
        and inner % (seq * seq_dev) == 0
        and col_dev % (inner // (seq * seq_dev)) == 0
        and seq * seq_dev * col_dev <= 1024
        and col * col_dev <= 512
    )


def solution(mesh):
    def choose(*args):
        seq_dev, col_dev, width = args[0].shape
        sizes = (mesh.shape["seq"], mesh.shape["col"], seq_dev, col_dev, width, args[1].shape[1])
        return (by_head if suits_by_head(*sizes) else on_device)(*args)

    return jax.shard_map(
        choose,
        mesh=mesh,
        in_specs=(P("seq", "col", None), P(), P(), P(), P(), P(), P(), P(), P()),
        out_specs=(P("seq", "col", None), P("seq", "col", None)),
        check_vma=False,
    )
```
